32 devices in a mesh: view: 4 (over y, core), row: 8 (over z, x).
Axes of the slice: x: 2, y: 2, z: 4, core: 2. Of those that a mesh axis runs over, the one named last changes fastest.
Arguments:
- features: float32 [4, 16384, 2048], P('view', 'row'), may hold values from -0.125 to 0.125
- view_maps: float32 [4, 2048, 256], P('view', 'row'), may hold values from -6 to 6
- shared: float32 [16384, 256], P('row'), may hold values from -6 to 6
Outputs:
- maps_out: float32 [4, 2048, 256], P('view', 'row')
- shared_out: float32 [16384, 256], P('row')
The draws below stay inside these ranges and needn't reach their ends.
All inputs are finite; a program needn't handle non-finite values.
Results may differ from the reference program's by a relative error of at most 0.00013.
Values sent between devices are 32-bit elements; how exact they have to be, the bound alone decides.
A program may use at most 128 MiB of HBM per device.

```python
import jax
import jax.numpy as jnp
from jax import lax

D = 2048
K = 256
ITERS = 2
NEWTON = 5
VIEWS = 4
TOTAL = 16384


def level_of(own_key, dims, split, smallest, top_value):
    def one(position, parts):
        heights = jax.random.uniform(jax.random.fold_in(jax.random.fold_in(own_key, 6), position), (parts,), jnp.float32, smallest / len(split), top_value / len(split))
        return jnp.repeat(jnp.exp(heights), dims[position] // parts).reshape((-1,) + (1,) * (len(dims) - position - 1))

    factor_of = one(*split[0])
    for cut in split[1:]:
        factor_of = factor_of * one(*cut)
    return factor_of


def centred(own_key, dims, scale, bound, split=(), kind=jnp.bfloat16):
    result = scale * jax.random.normal(own_key, dims, jnp.float32)
    if split:
        result = result * level_of(own_key, dims, split, -0.22, 0.18)
    return jnp.clip(result, -bound, bound).astype(kind)


def setup_inputs(seed: int = 0) -> dict:
    key_of = jax.random.split(jax.random.key(seed), 4)
    features = centred(key_of[0], (VIEWS, TOTAL, D), D ** -0.5, 0.125, ((0, 4), (1, 8)), jnp.float32)
    view_maps = centred(key_of[1], (VIEWS, D, K), 1.0, 6.0, ((0, 4), (1, 8)), jnp.float32)
    shared = centred(key_of[2], (TOTAL, K), 1.0, 6.0, ((0, 8),), jnp.float32)
    return {"features": features, "view_maps": view_maps, "shared": shared}


step_rate = 0.5

def newton_root(gram_matrix):
    highest = lax.Precision.HIGHEST
    frob_norm = jnp.sqrt(jnp.sum(gram_matrix * gram_matrix))
    scaled = gram_matrix / frob_norm
    identity = jnp.eye(gram_matrix.shape[0], dtype=jnp.float32)
    inverse_root = identity
    for newton_step in range(NEWTON):
        correction = 1.5 * identity - 0.5 * jnp.dot(inverse_root, scaled, precision=highest)
        scaled = jnp.dot(scaled, correction, precision=highest)
        inverse_root = jnp.dot(correction, inverse_root, precision=highest)
    return (inverse_root, frob_norm)

def reference(features, view_maps, shared):
    highest = lax.Precision.HIGHEST
    step_size = step_rate * D / TOTAL
    map_list = [view_maps[view_index] for view_index in range(VIEWS)]
    projected = [jnp.dot(features[view_index], map_list[view_index], precision=highest) for view_index in range(VIEWS)]
    for iteration in range(ITERS):
        for view_index in range(VIEWS):
            residual = projected[view_index] - shared
            gradient = jnp.dot(features[view_index].T, residual, precision=highest)
            map_list[view_index] = map_list[view_index] - step_size * gradient
            projected[view_index] = jnp.dot(features[view_index], map_list[view_index], precision=highest)
        summed = projected[0]
        for view_index in range(1, VIEWS):
            summed = summed + projected[view_index]
        average = summed / VIEWS
        gram_matrix = jnp.dot(average.T, average, precision=highest)
        inverse_root, frob_norm = newton_root(gram_matrix)
        shared = jnp.dot(average, inverse_root, precision=highest) * jnp.sqrt(TOTAL / frob_norm)
    return (jnp.stack(map_list, axis=0), shared)
```

```python
import functools
import math

import jax
import jax.numpy as jnp
from jax import lax
from jax.experimental import pallas as pl
from jax.experimental.pallas import tpu as pltpu
from jax.sharding import PartitionSpec as P

ITERS = 2
NEWTON = 5
STEP_RATE = 0.5
CORES = 2
LANES = 128
MESH = pl.DeviceIdType.MESH
F32 = jnp.float32
BF16 = jnp.bfloat16


def split(x):
    hi = x.astype(BF16)
    return hi, (x - hi.astype(F32)).astype(BF16)


def dot3s(a, b):
    lhs = jnp.concatenate([a[0], a[1], a[0]], axis=1)
    rhs = jnp.concatenate([b[0], b[0], b[1]], axis=0)
    return jnp.dot(lhs, rhs, preferred_element_type=F32)


def dot3(a, b):
    return dot3s(split(a), split(b))


def newton_steps(gram):
    size = gram.shape[0]
    frob = jnp.sqrt(jnp.sum(gram * gram, keepdims=True))
    scaled = gram / frob
    rows = lax.broadcasted_iota(jnp.int32, (size, size), 0)
    cols = lax.broadcasted_iota(jnp.int32, (size, size), 1)
    eye = jnp.where(rows == cols, 1.0, 0.0).astype(F32)
    root = None
    for step in range(NEWTON):
        ym = split(scaled)
        zy = scaled if root is None else dot3s(split(root), ym)
        corr = 1.5 * eye - 0.5 * zy
        cs = split(corr)
        if step < NEWTON - 1:
            scaled = dot3s(ym, cs)
        root = corr if root is None else dot3s(cs, split(root))
        yield root, frob


def kernel(
    dims,
    f_ref, w_ref, s_ref, wo_ref, so_ref,
    fhi, flo, fbuf, rthi, rtlo, y, wf, xs, xr, zs, zr,
    vs, cr, yr, av, gram, gr, gv, gfull,
    f_sem, agz_s, agz_r, agx_s, agx_r, rsx_s, rsx_r, rsz_s, rsz_r,
    vrc_s, vrc_r, vry_s, vry_r, vgy_s, vgy_r, vgc_s, vgc_r,
    g1_s, g1_r, g2_s, g2_r, g3_s, g3_r,
):
    nz, nx, ny, nc = dims
    nrow, nview = nz * nx, ny * nc
    row, view = lax.axis_index("row"), lax.axis_index("view")
    z, x = row // nx, row % nx
    yy, core = view // nc, view % nc
    local = y.shape[0]
    width = f_ref.shape[2]
    keys = y.shape[1]
    shard = w_ref.shape[1]
    total = local * nrow
    step_size = STEP_RATE * width / total
    chunk = fbuf.shape[1]
    nchunk = local // chunk
    part = local // nview
    gpart = keys // nrow
    cut, kp = wf.shape[2], wf.shape[4]
    sub = 512

    def at_row(zz, xx):
        return {"row": zz * nx + xx}

    def at_view(y1, c1):
        return {"view": y1 * nc + c1}

    def xmod(d):
        return lax.rem(x + d + nx, nx)

    def ymod(d):
        return lax.rem(yy + d + ny, ny)

    def cmod(d):
        return lax.rem(core + d + nc, nc)

    pending = []

    def remote(src, dst, ssem, rsem, dev):
        return pltpu.make_async_remote_copy(
            src_ref=src, dst_ref=dst, send_sem=ssem, recv_sem=rsem,
            device_id=dev, device_id_type=MESH,
        )

    def send(src, dst, ssem, rsem, dev):
        copy = remote(src, dst, ssem, rsem, dev)
        copy.start()
        pending.append(copy)

    def recv(buf, ssem, rsem, dev):
        remote(buf, buf, ssem, rsem, dev).wait_recv()

    def flush():
        for copy in pending:
            copy.wait_send()
        pending.clear()

    def line(j):
        low, high = z, nz - 1 - z
        m = jnp.minimum(low, high)
        near = j < 2 * m
        k = jnp.where(near, j // 2 + 1, j - m + 1)
        far_d = jnp.where(low > high, 1, -1)
        d = jnp.where(near, 1 - 2 * (j % 2), far_d)
        return z - d * k, d

    def inside(zz):
        return jnp.logical_and(zz >= 0, zz < nz)

    def load(c):
        return pltpu.make_async_copy(
            f_ref.at[0, pl.ds(c * chunk, chunk)], fbuf.at[c % 2], f_sem.at[c % 2]
        )

    load(0).start()
    for p in range(cut):
        wf[0, row, p] = w_ref[0, :, p * kp:(p + 1) * kp]
    barrier = pltpu.get_barrier_semaphore()
    for d in range(1, nrow):
        pl.semaphore_signal(
            barrier, inc=1, device_id={"row": lax.rem(row + d, nrow)}, device_id_type=MESH
        )
    for d in range(1, nview):
        pl.semaphore_signal(
            barrier, inc=1, device_id={"view": lax.rem(view + d, nview)}, device_id_type=MESH
        )
    pl.semaphore_wait(barrier, nrow + nview - 2)

    def ag_z(g, src, p, slot, to):
        ref = wf.at[g % 2, src * nx + x, p]
        return remote(ref, ref, agz_s.at[g, slot, p], agz_r.at[g, src, p], at_row(to, x))

    def ag_x(g, src, dx, p):
        ref = wf.at[g % 2, src * nx + x, p]
        return remote(
            ref, ref, agx_s.at[g, src, dx, p], agx_r.at[g, src, dx, p], at_row(z, xmod(dx))
        )

    def ag_own(g, p):
        @pl.when(z + 1 < nz)
        def _():
            ag_z(g, z, p, z, z + 1).start()

        @pl.when(z > 0)
        def _():
            ag_z(g, z, p, nz, z - 1).start()

        for dx in range(1, nx):
            ag_x(g, z, dx, p).start()

    def ag_event(g, j, p):
        src, d = line(j)
        ag_z(g, src, p, src, z - d).wait_recv()

        @pl.when(inside(z + d))
        def _():
            ag_z(g, src, p, src, z + d).start()

        for dx in range(1, nx):
            ag_x(g, src, dx, p).start()

    def ag_cross(g, src):
        for dx in range(1, nx):
            block = src * nx + xmod(-dx)
            for p in range(cut):
                recv(
                    wf.at[g % 2, block, p],
                    agx_s.at[g, src, dx, p], agx_r.at[g, src, dx, p], at_row(z, xmod(-dx)),
                )
            project(g, block, False)

    def ag_flush(g):
        for p in range(cut):
            @pl.when(z + 1 < nz)
            def _():
                ag_z(g, z, p, z, z + 1).wait_send()

            @pl.when(z > 0)
            def _():
                ag_z(g, z, p, nz, z - 1).wait_send()

            for dx in range(1, nx):
                ag_x(g, z, dx, p).wait_send()

        @pl.loop(0, nz - 1)
        def _(j):
            src, d = line(j)
            for p in range(cut):
                @pl.when(inside(z + d))
                def _():
                    ag_z(g, src, p, src, z + d).wait_send()

                for dx in range(1, nx):
                    ag_x(g, src, dx, p).wait_send()

    def project(g, block, first):
        wb = jnp.concatenate([wf[g % 2, block, p] for p in range(cut)], axis=1)
        ws = split(wb)
        rhs = jnp.concatenate([ws[0], ws[0], ws[1]], axis=0)

        @pl.loop(0, local // sub)
        def _(c):
            rows = pl.ds(pl.multiple_of(c * sub, sub), sub)
            hi, lo = fhi[block, rows], flo[block, rows]
            out = jnp.dot(
                jnp.concatenate([hi, lo, hi], axis=1), rhs, preferred_element_type=F32
            )
            if first:
                y[rows] = out
            else:
                y[rows] += out

    def ag_run(g, started):
        project(g, row, True)
        if not started:
            for p in range(cut):
                ag_event(g, 0, p)

        @pl.loop(0, nz - 1)
        def _(j):
            src, _ = line(j)
            project(g, src * nx + x, False)

            @pl.when(j + 1 < nz - 1)
            def _():
                for p in range(cut):
                    ag_event(g, j + 1, p)

            ag_cross(g, jnp.where(j == 0, z, line(j - 1)[0]))

        ag_cross(g, line(nz - 2)[0])

    def put_rt(rows, value):
        hi, lo = split(value.T)
        rthi[:, rows] = hi
        rtlo[:, rows] = lo

    def gradient(block):
        hi, lo = fhi[block], flo[block]
        rh = rthi[...]
        out = jnp.dot(rh, hi, preferred_element_type=F32)
        out += jnp.dot(rh, lo, preferred_element_type=F32)
        out += jnp.dot(rtlo[...], hi, preferred_element_type=F32)
        return out.reshape(cut, kp, shard)

    def order(i):
        return jnp.where(i == nz - 1, z, line(nz - 2 - i)[0])

    def rs_x(r, t, dx, p):
        return remote(
            xs.at[r % 2, t, dx - 1, p], xr.at[r % 2, t, dx - 1, p],
            rsx_s.at[r, t, dx, p], rsx_r.at[r, t, dx, p], at_row(z, xmod(dx)),
        )

    def rs_z(r, t, d, p):
        slot = jnp.where(jnp.logical_and(d < 0, t == z - d), nz, t)
        return remote(
            zs.at[r % 2, t, p], zr.at[r % 2, slot, p],
            rsz_s.at[r, t, p], rsz_r.at[r, slot, p], at_row(z - d, x),
        )

    def rs_compute(r):
        @pl.loop(0, nz)
        def _(i):
            t = order(i)
            for dx in range(1, nx):
                xs[r % 2, t, dx - 1] = gradient(t * nx + xmod(dx))
                for p in range(cut):
                    rs_x(r, t, dx, p).start()

        @pl.loop(0, nz)
        def _(i):
            t = order(i)
            zs[r % 2, t] = gradient(t * nx + x)

    def rs_over_x(r, t, p):
        acc = zs[r % 2, t, p]
        for dx in range(1, nx):
            recv(
                xr.at[r % 2, t, dx - 1, p],
                rsx_s.at[r, t, dx, p], rsx_r.at[r, t, dx, p], at_row(z, xmod(-dx)),
            )
            acc = acc + xr[r % 2, t, dx - 1, p]
        return acc

    def rs_take(r, t, slot, p, frm):
        recv(
            zr.at[r % 2, slot, p], rsz_s.at[r, t, p], rsz_r.at[r, slot, p], at_row(frm, x)
        )
        zs[r % 2, t, p] += zr[r % 2, slot, p]

    def rs_event(r, j, p):
        t, d = line(j)
        zs[r % 2, t, p] = rs_over_x(r, t, p)

        @pl.when(inside(z + d))
        def _():
            rs_take(r, t, t, p, z + d)

        rs_z(r, t, d, p).start()

    def rs_own(r, p):
        zs[r % 2, z, p] = rs_over_x(r, z, p)

        @pl.when(z + 1 < nz)
        def _():
            rs_take(r, z, z, p, z + 1)

        @pl.when(z > 0)
        def _():
            rs_take(r, z, nz, p, z - 1)

        return zs[r % 2, z, p]

    def rs_flush(r):
        @pl.loop(0, nz)
        def _(i):
            t = order(i)
            for dx in range(1, nx):
                for p in range(cut):
                    rs_x(r, t, dx, p).wait_send()

        @pl.loop(0, nz - 1)
        def _(j):
            t, d = line(j)
            for p in range(cut):
                rs_z(r, t, d, p).wait_send()

    def yblock(block):
        return pl.ds(pl.multiple_of(block * part, part), part)

    def view_send(it):
        for dy in list(range(1, ny)) + [0]:
            for dc in range(1, nc):
                ct = cmod(dc)
                send(
                    y.at[yblock(ymod(dy) * nc + ct)], cr.at[it, dy, dc - 1],
                    vrc_s.at[it, dy, dc], vrc_r.at[it, dy, dc], at_view(yy, ct),
                )

    def view_mid(it):
        for dy in list(range(1, ny)) + [0]:
            acc = y[yblock(ymod(dy) * nc + core)]
            for dc in range(1, nc):
                recv(
                    cr.at[it, dy, dc - 1], vrc_s.at[it, dy, dc], vrc_r.at[it, dy, dc],
                    at_view(yy, cmod(-dc)),
                )
                acc = acc + cr[it, dy, dc - 1]
            vs[it, dy] = acc
            if dy:
                send(
                    vs.at[it, dy], yr.at[it, dy], vry_s.at[it, dy], vry_r.at[it, dy],
                    at_view(ymod(dy), core),
                )

    def view_end(it):
        acc = vs[it, 0]
        for dy in range(1, ny):
            recv(
                yr.at[it, dy], vry_s.at[it, dy], vry_r.at[it, dy],
                at_view(ymod(-dy), core),
            )
            acc = acc + yr[it, dy]
        av[it, view] = acc / nview
        own = av.at[it, view]
        for dy in range(1, ny):
            send(
                own, own, vgy_s.at[it, dy], vgy_r.at[it, dy], at_view(ymod(dy), core)
            )
        for dc in range(1, nc):
            send(
                own, own, vgc_s.at[it, 0, dc], vgc_r.at[it, 0, dc], at_view(yy, cmod(dc))
            )

    def gram_start(it):
        own = av[it, view]
        hi, lo = split(own)
        thi, tlo = split(own.T)
        gram[it] = dot3s((thi, tlo), (hi, lo)).reshape(nrow, gpart, keys)
        for d in range(1, nrow):
            to = lax.rem(row + d, nrow)
            send(
                gram.at[it, to], gr.at[it, d], g1_s.at[it, d], g1_r.at[it, d], {"row": to}
            )

    def gram_views(it):
        acc = gram[it, row]
        for d in range(1, nrow):
            recv(
                gr.at[it, d], g1_s.at[it, d], g1_r.at[it, d],
                {"row": lax.rem(row - d + nrow, nrow)},
            )
            acc = acc + gr[it, d]
        gv[it, 0] = acc
        for d in range(1, nview):
            send(
                gv.at[it, 0], gv.at[it, d], g2_s.at[it, d], g2_r.at[it, d],
                {"view": lax.rem(view + d, nview)},
            )

    def gram_rows(it):
        acc = gv[it, 0]
        for d in range(1, nview):
            recv(
                gv.at[it, d], g2_s.at[it, d], g2_r.at[it, d],
                {"view": lax.rem(view - d + nview, nview)},
            )
            acc = acc + gv[it, d]
        gfull[it, row] = acc
        mine = gfull.at[it, row]
        for d in range(1, nrow):
            send(
                mine, mine, g3_s.at[it, d], g3_r.at[it, d],
                {"row": lax.rem(row + d, nrow)},
            )

    def gram_end(it):
        for d in range(1, nrow):
            src = lax.rem(row - d + nrow, nrow)
            recv(gfull.at[it, src], g3_s.at[it, d], g3_r.at[it, d], {"row": src})
        return newton_steps(gfull[it].reshape(keys, keys))

    def forward_average(it):
        for dy in range(1, ny):
            ysrc = ymod(-dy)
            got = av.at[it, ysrc * nc + core]
            recv(got, vgy_s.at[it, dy], vgy_r.at[it, dy], at_view(ysrc, core))
            for dc in range(1, nc):
                send(
                    got, got, vgc_s.at[it, dy, dc], vgc_r.at[it, dy, dc],
                    at_view(yy, cmod(dc)),
                )

    def finish_average(it):
        for dy in range(ny):
            for dc in range(1, nc):
                csrc = cmod(-dc)
                recv(
                    av.at[it, ymod(-dy) * nc + csrc],
                    vgc_s.at[it, dy, dc], vgc_r.at[it, dy, dc], at_view(yy, csrc),
                )

    far = nz - 2
    ns = jax.named_scope
    with ns("q_load"):
        for p in range(cut):
            ag_own(0, p)
        for c in range(nchunk):
            if c + 1 < nchunk:
                load(c + 1).start()
            load(c).wait()
            for b in range(nrow):
                hi, lo = split(fbuf[c % 2, :, b * shard:(b + 1) * shard])
                fhi[b, c * chunk:(c + 1) * chunk] = hi
                flo[b, c * chunk:(c + 1) * chunk] = lo
            if nchunk - c <= cut:
                ag_event(0, 0, cut - nchunk + c)
    with ns("q_ag0"):
        ag_run(0, True)
    with ns("q_res"):
        for c in range(local // sub):
            rows = slice(c * sub, (c + 1) * sub)
            put_rt(rows, y[rows] - s_ref[rows])
    with ns("q_rs0c"):
        rs_compute(0)
    with ns("q_rs0e"):
        @pl.loop(0, nz - 1)
        def _(i):
            for p in range(cut):
                rs_event(0, far - i, p)
        for p in range(cut):
            wf[1, row, p] = wf[0, row, p] - step_size * rs_own(0, p).T
            ag_own(1, p)
    with ns("q_fl"):
        ag_flush(0)
        rs_flush(0)
    with ns("q_ag1"):
        ag_run(1, False)
    with ns("q_vsend"):
        view_send(0)
        for c in range(local // sub):
            rows = slice(c * sub, (c + 1) * sub)
            put_rt(rows, y[rows])
    with ns("q_vmid"):
        view_mid(0)
    with ns("q_rs1c"):
        rs_compute(1)
    with ns("q_rs1e"):
        for p in range(cut):
            rs_event(1, far, p)
    with ns("q_vend"):
        view_end(0)
    with ns("q_g1"):
        gram_start(0)
    with ns("q_rs1e"):
        @pl.loop(1, nz - 1)
        def _(i):
            for p in range(cut):
                rs_event(1, far - i, p)
        for p in range(cut):
            rs_own(1, p)
    with ns("q_g2"):
        gram_views(0)
    with ns("q_fa"):
        forward_average(0)
    with ns("q_g3"):
        gram_rows(0)
    with ns("q_fin"):
        finish_average(0)
        ag_flush(1)
        rs_flush(1)
        for v in range(nview):
            put_rt(slice(v * part, (v + 1) * part), av[0, v])
    with ns("q_rs2c"):
        rs_compute(2)
    with ns("q_rs2e"):
        for p in range(cut):
            rs_event(2, far, p)
    with ns("q_nw"):
        steps = gram_end(0)
        next(steps)
        root, frob = next(steps)
    with ns("q_rs2e"):
        for i in range(1, nz - 1):
            for p in range(cut):
                rs_event(2, far - i, p)
            root, frob = next(steps, (root, frob))
        for root, frob in steps:
            pass
        for p in range(cut):
            rs_own(2, p)
    with ns("q_w2"):
        scale = jnp.sqrt(total / frob)
        moved = dot3s(split(zs[0, z].reshape(keys, shard).T), split(root)) * scale
        moved = step_size * (zs[1, z].reshape(keys, shard).T - moved)
        for p in range(cut):
            wf[0, row, p] = wf[1, row, p] - moved[:, p * kp:(p + 1) * kp]
            ag_own(2, p)
        flush()
        rs_flush(2)
    with ns("q_ag2"):
        ag_run(2, False)
    with ns("q_vmid"):
        view_send(1)
        view_mid(1)
        for p in range(cut):
            wo_ref[0, :, p * kp:(p + 1) * kp] = wf[0, row, p]
    with ns("q_vend"):
        view_end(1)
    with ns("q_g1"):
        gram_start(1)
        gram_views(1)
    with ns("q_g3"):
        gram_rows(1)
        ag_flush(2)
        forward_average(1)
    with ns("q_g4"):
        steps = gram_end(1)
    with ns("q_nw"):
        for root, frob in steps:
            pass
        scale = jnp.sqrt(total / frob)
    with ns("q_fina"):
        finish_average(1)
    with ns("q_out"):
        rs = split(root)
        for v in range(nview):
            so_ref[v * part:(v + 1) * part] = dot3s(split(av[1, v]), rs) * scale
        flush()


def solution(mesh):
    nrow, nview = mesh.shape["row"], mesh.shape["view"]
    nx = max(d for d in range(1, math.isqrt(nrow) + 1) if nrow % d == 0)
    nz = nrow // nx
    nc = CORES if nview % CORES == 0 else 1
    ny = nview // nc

    def local(features, view_maps, shared):
        rows, width = features.shape[1], features.shape[2]
        shard, keys = view_maps.shape[1], view_maps.shape[2]
        part, gpart = rows // nview, keys // nrow
        cut = max(1, keys // LANES)
        kp = keys // cut
        chunk = 256
        dma = pltpu.SemaphoreType.DMA
        sems = []
        for shape in [
            (3, nz + 1, cut), (3, nz, nx, cut), (3, nz, nx, cut), (3, nz + 1, cut),
            (ITERS, ny, nc), (ITERS, ny), (ITERS, ny), (ITERS, ny, nc),
            (ITERS, nrow), (ITERS, nview), (ITERS, nrow),
        ]:
            sems += [dma(shape), dma(shape)]
        vmem = pl.BlockSpec(memory_space=pltpu.VMEM)
        return pl.pallas_call(
            functools.partial(kernel, (nz, nx, ny, nc)),
            out_shape=(
                jax.ShapeDtypeStruct(view_maps.shape, F32),
                jax.ShapeDtypeStruct(shared.shape, F32),
            ),
            in_specs=[pl.BlockSpec(memory_space=pl.ANY), vmem, vmem],
            out_specs=(vmem, vmem),
            scratch_shapes=[
                pltpu.VMEM((nrow, rows, shard), BF16),
                pltpu.VMEM((nrow, rows, shard), BF16),
                pltpu.VMEM((2, chunk, width), F32),
                pltpu.VMEM((keys, rows), BF16),
                pltpu.VMEM((keys, rows), BF16),
                pltpu.VMEM((rows, keys), F32),
                pltpu.VMEM((2, nrow, cut, shard, kp), F32),
                pltpu.VMEM((2, nz, nx - 1, cut, kp, shard), F32),
                pltpu.VMEM((2, nz, nx - 1, cut, kp, shard), F32),
                pltpu.VMEM((2, nz, cut, kp, shard), F32),
                pltpu.VMEM((2, nz + 1, cut, kp, shard), F32),
                pltpu.VMEM((ITERS, ny, part, keys), F32),
                pltpu.VMEM((ITERS, ny, nc - 1, part, keys), F32),
                pltpu.VMEM((ITERS, ny, part, keys), F32),
                pltpu.VMEM((ITERS, nview, part, keys), F32),
                pltpu.VMEM((ITERS, nrow, gpart, keys), F32),
                pltpu.VMEM((ITERS, nrow, gpart, keys), F32),
                pltpu.VMEM((ITERS, nview, gpart, keys), F32),
                pltpu.VMEM((ITERS, nrow, gpart, keys), F32),
                dma((2,)),
            ] + sems,
            compiler_params=pltpu.CompilerParams(
                collective_id=0, has_side_effects=True, vmem_limit_bytes=67043328
            ),
        )(features, view_maps, shared)

    in_specs = (P("view", "row", None), P("view", "row", None), P("row", None))
    out_specs = (P("view", "row", None), P("row", None))
    return jax.shard_map(local, mesh=mesh, in_specs=in_specs, out_specs=out_specs, check_vma=False)
```

```python
import functools
import math

import jax
import jax.numpy as jnp
from jax import lax
from jax.experimental import pallas as pl
from jax.experimental.pallas import tpu as pltpu
from jax.sharding import PartitionSpec as P

ITERS = 2
NEWTON = 5
STEP_RATE = 0.5
CORES = 2
SUBLANES = 8
HALVES = 2
CUT = 2
LATE = 0
MESH = pl.DeviceIdType.MESH
F32 = jnp.float32
BF16 = jnp.bfloat16


def split(x):
    hi = x.astype(BF16)
    return hi, (x - hi.astype(F32)).astype(BF16)


def dot3s(a, b):
    lhs = jnp.concatenate([a[0], a[1], a[0]], axis=1)
    rhs = jnp.concatenate([b[0], b[0], b[1]], axis=0)
    return jnp.dot(lhs, rhs, preferred_element_type=F32)


def dot3(a, b):
    return dot3s(split(a), split(b))


def newton_steps(gram):
    size = gram.shape[0]
    frob = jnp.sqrt(jnp.sum(gram * gram, keepdims=True))
    scaled = gram / frob
    rows = lax.broadcasted_iota(jnp.int32, (size, size), 0)
    cols = lax.broadcasted_iota(jnp.int32, (size, size), 1)
    eye = jnp.where(rows == cols, 1.0, 0.0).astype(F32)
    root = None
    for step in range(NEWTON):
        ym = split(scaled)
        zy = scaled if root is None else dot3s(split(root), ym)
        corr = 1.5 * eye - 0.5 * zy
        cs = split(corr)
        if step < NEWTON - 1:
            scaled = dot3s(ym, cs)
        root = corr if root is None else dot3s(cs, split(root))
        yield root, frob


def kernel(
    dims, pieces, cross,
    f_ref, w_ref, s_ref, wo_ref, so_ref,
    fhi, flo, fbuf, rthi, rtlo, y, wf, xs, xr, zs, zr, xq, zq,
    vs, cr, yr, av, gram, gr, gv, gfull,
    f_sem, agz_s, agz_r, agx_s, agx_r, rsx_s, rsx_r, rsz_s, rsz_r, rsq_s, rsq_r, rsxq_s, rsxq_r,
    vrc_s, vrc_r, vry_s, vry_r, vgy_s, vgy_r, vgc_s, vgc_r,
    g1_s, g1_r, g2_s, g2_r, g3_s, g3_r,
):
    nz, nx, ny, nc = dims
    nrow, nview = nz * nx, ny * nc
    row, view = lax.axis_index("row"), lax.axis_index("view")
    z, x = row // nx, row % nx
    yy, core = view // nc, view % nc
    local = y.shape[0]
    width = f_ref.shape[2]
    keys = y.shape[1]
    shard = w_ref.shape[1]
    total = local * nrow
    step_size = STEP_RATE * width / total
    chunk = fbuf.shape[1]
    nchunk = local // chunk
    part = local // nview
    gpart = keys // nrow
    cut = len(pieces)
    rows_of = [pl.ds(a, n) for a, n in pieces]
    crows = pl.ds(*cross)
    late = cross[1] > 0
    ends = range(cut + 1) if late else range(cut)
    rels = list(range(nx)) if late else []
    sub = 512

    def at_row(zz, xx):
        return {"row": zz * nx + xx}

    def at_view(y1, c1):
        return {"view": y1 * nc + c1}

    def xmod(d):
        return lax.rem(x + d + nx, nx)

    def ymod(d):
        return lax.rem(yy + d + ny, ny)

    def cmod(d):
        return lax.rem(core + d + nc, nc)

    pending = []

    def remote(src, dst, ssem, rsem, dev):
        return pltpu.make_async_remote_copy(
            src_ref=src, dst_ref=dst, send_sem=ssem, recv_sem=rsem,
            device_id=dev, device_id_type=MESH,
        )

    def send(src, dst, ssem, rsem, dev):
        copy = remote(src, dst, ssem, rsem, dev)
        copy.start()
        pending.append(copy)

    def recv(buf, ssem, rsem, dev):
        remote(buf, buf, ssem, rsem, dev).wait_recv()

    def flush():
        for copy in pending:
            copy.wait_send()
        pending.clear()

    def line(j):
        low, high = z, nz - 1 - z
        m = jnp.minimum(low, high)
        near = j < 2 * m
        k = jnp.where(near, j // 2 + 1, j - m + 1)
        far_d = jnp.where(low > high, 1, -1)
        d = jnp.where(near, 1 - 2 * (j % 2), far_d)
        return z - d * k, d

    def inside(zz):
        return jnp.logical_and(zz >= 0, zz < nz)

    def load(c):
        return pltpu.make_async_copy(
            f_ref.at[0, pl.ds(c * chunk, chunk)], fbuf.at[c % 2], f_sem.at[c % 2]
        )

    load(0).start()
    wf[0, row] = w_ref[0].T
    barrier = pltpu.get_barrier_semaphore()
    for d in range(1, nrow):
        pl.semaphore_signal(
            barrier, inc=1, device_id={"row": lax.rem(row + d, nrow)}, device_id_type=MESH
        )
    for d in range(1, nview):
        pl.semaphore_signal(
            barrier, inc=1, device_id={"view": lax.rem(view + d, nview)}, device_id_type=MESH
        )
    pl.semaphore_wait(barrier, nrow + nview - 2)

    def ag_z(g, src, p, rel, slot, to):
        rows = crows if p == cut else rows_of[p]
        ref = wf.at[g % 2, src * nx + xmod(rel), rows]
        return remote(
            ref, ref, agz_s.at[g, slot, p + rel], agz_r.at[g, src, p + rel], at_row(to, x)
        )

    def ag_x(g, src, dx, p):
        rows = crows if p == cut else rows_of[p]
        ref = wf.at[g % 2, src * nx + x, rows]
        return remote(
            ref, ref, agx_s.at[g, src, dx, p], agx_r.at[g, src, dx, p], at_row(z, xmod(dx))
        )

    def ag_both(g, p, rel, wait=False):
        @pl.when(z + 1 < nz)
        def _():
            copy = ag_z(g, z, p, rel, z, z + 1)
            copy.wait_send() if wait else copy.start()

        @pl.when(z > 0)
        def _():
            copy = ag_z(g, z, p, rel, nz, z - 1)
            copy.wait_send() if wait else copy.start()

    def ag_own(g, p):
        if p == cut:
            for dx in range(1, nx):
                ag_x(g, z, dx, p).start()
            ag_both(g, p, 0)
        else:
            ag_both(g, p, 0)
            for dx in range(1, nx):
                ag_x(g, z, dx, p).start()

    def ag_crossed(g):
        for dx in rels[1:]:
            recv(
                wf.at[g % 2, z * nx + xmod(-dx), crows],
                agx_s.at[g, z, dx, cut], agx_r.at[g, z, dx, cut], at_row(z, xmod(-dx)),
            )
            ag_both(g, cut, nx - dx)

    def ag_relay(g, j, p, rel, wait=False):
        src, d = line(j)
        if not wait:
            ag_z(g, src, p, rel, src, z - d).wait_recv()

        @pl.when(inside(z + d))
        def _():
            copy = ag_z(g, src, p, rel, src, z + d)
            copy.wait_send() if wait else copy.start()

    def ag_event(g, j, p):
        ag_relay(g, j, p, 0)
        for dx in range(1, nx):
            ag_x(g, line(j)[0], dx, p).start()

    def ag_last(g, src):
        for dx in range(1, nx):
            block = src * nx + xmod(-dx)
            for p in range(cut):
                recv(
                    wf.at[g % 2, block, rows_of[p]],
                    agx_s.at[g, src, dx, p], agx_r.at[g, src, dx, p], at_row(z, xmod(-dx)),
                )
            project(g, block, False)

    def ag_flush(g):
        for p in ends:
            ag_both(g, p, 0, True)
            for dx in range(1, nx):
                ag_x(g, z, dx, p).wait_send()
        for rel in rels[1:]:
            ag_both(g, cut, rel, True)

        @pl.loop(0, nz - 1)
        def _(j):
            for p in range(cut):
                ag_relay(g, j, p, 0, True)
                for dx in range(1, nx):
                    ag_x(g, line(j)[0], dx, p).wait_send()
            for rel in rels:
                ag_relay(g, j, cut, rel, True)

    def project(g, block, first):
        hi, lo = split(wf[g % 2, block])
        rhs = jnp.concatenate([hi, hi, lo], axis=1)

        @pl.loop(0, local // sub)
        def _(c):
            rows = pl.ds(pl.multiple_of(c * sub, sub), sub)
            fh, fl = fhi[block, rows], flo[block, rows]
            out = lax.dot_general(
                jnp.concatenate([fh, fl, fh], axis=1), rhs, (((1,), (1,)), ((), ())),
                preferred_element_type=F32,
            )
            if first:
                y[rows] = out
            else:
                y[rows] += out

    def ag_run(g, started):
        if not started:
            project(g, row, True)
            for p in range(cut):
                ag_event(g, 0, p)
            ag_crossed(g)
        else:
            project(g, row, True)

        @pl.loop(0, nz - 1)
        def _(j):
            @pl.when(j + 1 < nz - 1)
            def _():
                for p in range(cut):
                    ag_event(g, j + 1, p)

            for rel in rels:
                ag_relay(g, j, cut, rel)
            project(g, line(j)[0] * nx + x, False)
            ag_last(g, jnp.where(j == 0, z, line(j - 1)[0]))

        ag_last(g, line(nz - 2)[0])

    def put_rt(rows, value):
        hi, lo = split(value.T)
        rthi[:, rows] = hi
        rtlo[:, rows] = lo

    def gradient(block):
        hi, lo = fhi[block], flo[block]
        rh = rthi[...]
        out = jnp.dot(rh, hi, preferred_element_type=F32)
        out += jnp.dot(rh, lo, preferred_element_type=F32)
        out += jnp.dot(rtlo[...], hi, preferred_element_type=F32)
        return out

    def order(i):
        return jnp.where(i == nz - 1, z, line(nz - 2 - i)[0])

    def rs_x(r, t, dx, p):
        return remote(
            xs.at[r % 2, t, dx - 1, rows_of[p]], xr.at[r % 2, t, dx - 1, rows_of[p]],
            rsx_s.at[r, t, dx, p], rsx_r.at[r, t, dx, p], at_row(z, xmod(dx)),
        )

    def slot_of(t, d):
        return jnp.where(jnp.logical_and(d < 0, t == z - d), nz, t)

    def rs_z(r, t, d, p):
        slot = slot_of(t, d)
        return remote(
            zs.at[r % 2, t, rows_of[p]], zr.at[r % 2, slot, rows_of[p]],
            rsz_s.at[r, t, p], rsz_r.at[r, slot, p], at_row(z - d, x),
        )

    def mine(r, t, rel):
        return zs.at[r % 2, t, crows] if rel == 0 else xs.at[r % 2, t, rel - 1, crows]

    def rs_q(r, t, d, rel):
        slot = slot_of(t, d)
        return remote(
            mine(r, t, rel), zq.at[r % 2, slot, rel],
            rsq_s.at[r, t, rel], rsq_r.at[r, slot, rel], at_row(z - d, x),
        )

    def rs_qx(r, rel):
        return remote(
            mine(r, z, rel), xq.at[r % 2, rel - 1],
            rsxq_s.at[r, rel], rsxq_r.at[r, rel], at_row(z, xmod(rel)),
        )

    def rs_first(r, i):
        t = order(i)
        for dx in range(1, nx):
            xs[r % 2, t, dx - 1] = gradient(t * nx + xmod(dx))
            for p in range(cut):
                rs_x(r, t, dx, p).start()

    def rs_compute(r, begun=0):
        @pl.loop(begun, nz)
        def _(i):
            rs_first(r, i)

        @pl.loop(0, nz)
        def _(i):
            t = order(i)
            zs[r % 2, t] = gradient(t * nx + x)

    def rs_over_x(r, t, p):
        acc = zs[r % 2, t, rows_of[p]]
        for dx in range(1, nx):
            recv(
                xr.at[r % 2, t, dx - 1, rows_of[p]],
                rsx_s.at[r, t, dx, p], rsx_r.at[r, t, dx, p], at_row(z, xmod(-dx)),
            )
            acc = acc + xr[r % 2, t, dx - 1, rows_of[p]]
        return acc

    def rs_take(r, t, slot, p, frm):
        recv(
            zr.at[r % 2, slot, rows_of[p]], rsz_s.at[r, t, p], rsz_r.at[r, slot, p],
            at_row(frm, x),
        )
        zs[r % 2, t, rows_of[p]] += zr[r % 2, slot, rows_of[p]]

    def rs_qtake(r, t, slot, rel, frm):
        recv(
            zq.at[r % 2, slot, rel], rsq_s.at[r, t, rel], rsq_r.at[r, slot, rel],
            at_row(frm, x),
        )
        mine(r, t, rel)[...] += zq[r % 2, slot, rel]

    def rs_event(r, j):
        t, d = line(j)
        for rel in rels:
            @pl.when(inside(z + d))
            def _():
                rs_qtake(r, t, t, rel, z + d)

            rs_q(r, t, d, rel).start()
        for p in range(cut):
            zs[r % 2, t, rows_of[p]] = rs_over_x(r, t, p)

            @pl.when(inside(z + d))
            def _():
                rs_take(r, t, t, p, z + d)

            rs_z(r, t, d, p).start()

    def rs_cross(r):
        for rel in rels[1:] + rels[:1]:
            @pl.when(z + 1 < nz)
            def _():
                rs_qtake(r, z, z, rel, z + 1)

            @pl.when(z > 0)
            def _():
                rs_qtake(r, z, nz, rel, z - 1)

            if rel:
                rs_qx(r, rel).start()

    def rs_own(r, p):
        if p == cut:
            acc = zs[r % 2, z, crows]
            for dx in range(1, nx):
                recv(
                    xq.at[r % 2, dx - 1], rsxq_s.at[r, dx], rsxq_r.at[r, dx],
                    at_row(z, xmod(-dx)),
                )
                acc = acc + xq[r % 2, dx - 1]
            zs[r % 2, z, crows] = acc
            return acc
        zs[r % 2, z, rows_of[p]] = rs_over_x(r, z, p)

        @pl.when(z + 1 < nz)
        def _():
            rs_take(r, z, z, p, z + 1)

        @pl.when(z > 0)
        def _():
            rs_take(r, z, nz, p, z - 1)

        return zs[r % 2, z, rows_of[p]]

    def rs_flush(r):
        @pl.loop(0, nz)
        def _(i):
            t = order(i)
            for dx in range(1, nx):
                for p in range(cut):
                    rs_x(r, t, dx, p).wait_send()

        @pl.loop(0, nz - 1)
        def _(j):
            t, d = line(j)
            for p in range(cut):
                rs_z(r, t, d, p).wait_send()
            for rel in rels:
                rs_q(r, t, d, rel).wait_send()

        for rel in rels[1:]:
            rs_qx(r, rel).wait_send()

    half = part // HALVES
    halves = [pl.ds(h * half, half) for h in range(HALVES)]

    def yblock(block, h):
        return pl.ds(pl.multiple_of(block * part + h * half, half), half)

    def view_send(it):
        for dy in list(range(1, ny)) + [0]:
            for h in range(HALVES):
                for dc in range(1, nc):
                    ct = cmod(dc)
                    send(
                        y.at[yblock(ymod(dy) * nc + ct, h)], cr.at[it, dy, dc - 1, halves[h]],
                        vrc_s.at[it, dy, dc, h], vrc_r.at[it, dy, dc, h], at_view(yy, ct),
                    )

    def view_mid(it):
        for dy in list(range(1, ny)) + [0]:
            for h in range(HALVES):
                acc = y[yblock(ymod(dy) * nc + core, h)]
                for dc in range(1, nc):
                    recv(
                        cr.at[it, dy, dc - 1, halves[h]],
                        vrc_s.at[it, dy, dc, h], vrc_r.at[it, dy, dc, h],
                        at_view(yy, cmod(-dc)),
                    )
                    acc = acc + cr[it, dy, dc - 1, halves[h]]
                vs[it, dy, halves[h]] = acc
                if dy:
                    send(
                        vs.at[it, dy, halves[h]], yr.at[it, dy, halves[h]],
                        vry_s.at[it, dy, h], vry_r.at[it, dy, h], at_view(ymod(dy), core),
                    )

    def view_end(it, h):
        acc = vs[it, 0, halves[h]]
        for dy in range(1, ny):
            recv(
                yr.at[it, dy, halves[h]], vry_s.at[it, dy, h], vry_r.at[it, dy, h],
                at_view(ymod(-dy), core),
            )
            acc = acc + yr[it, dy, halves[h]]
        av[it, view, halves[h]] = acc / nview
        own = av.at[it, view, halves[h]]
        for dy in range(1, ny):
            send(
                own, own, vgy_s.at[it, dy, h], vgy_r.at[it, dy, h], at_view(ymod(dy), core)
            )
        for dc in range(1, nc):
            send(
                own, own, vgc_s.at[it, 0, dc, h], vgc_r.at[it, 0, dc, h],
                at_view(yy, cmod(dc)),
            )

    def gram_start(it):
        own = av[it, view]
        hi, lo = split(own)
        thi, tlo = split(own.T)
        gram[it] = dot3s((thi, tlo), (hi, lo)).reshape(nrow, gpart, keys)
        for d in range(1, nrow):
            to = lax.rem(row + d, nrow)
            send(
                gram.at[it, to], gr.at[it, d], g1_s.at[it, d], g1_r.at[it, d], {"row": to}
            )

    def gram_views(it):
        acc = gram[it, row]
        for d in range(1, nrow):
            recv(
                gr.at[it, d], g1_s.at[it, d], g1_r.at[it, d],
                {"row": lax.rem(row - d + nrow, nrow)},
            )
            acc = acc + gr[it, d]
        gv[it, 0] = acc
        for d in range(1, nview):
            send(
                gv.at[it, 0], gv.at[it, d], g2_s.at[it, d], g2_r.at[it, d],
                {"view": lax.rem(view + d, nview)},
            )

    def gram_rows(it):
        acc = gv[it, 0]
        for d in range(1, nview):
            recv(
                gv.at[it, d], g2_s.at[it, d], g2_r.at[it, d],
                {"view": lax.rem(view - d + nview, nview)},
            )
            acc = acc + gv[it, d]
        gfull[it, row] = acc
        mine = gfull.at[it, row]
        for d in range(1, nrow):
            send(
                mine, mine, g3_s.at[it, d], g3_r.at[it, d],
                {"row": lax.rem(row + d, nrow)},
            )

    def gram_end(it):
        for d in range(1, nrow):
            src = lax.rem(row - d + nrow, nrow)
            recv(gfull.at[it, src], g3_s.at[it, d], g3_r.at[it, d], {"row": src})
        return newton_steps(gfull[it].reshape(keys, keys))

    def forward_average(it, h):
        for dy in range(1, ny):
            ysrc = ymod(-dy)
            got = av.at[it, ysrc * nc + core, halves[h]]
            recv(got, vgy_s.at[it, dy, h], vgy_r.at[it, dy, h], at_view(ysrc, core))
            for dc in range(1, nc):
                send(
                    got, got, vgc_s.at[it, dy, dc, h], vgc_r.at[it, dy, dc, h],
                    at_view(yy, cmod(dc)),
                )

    def finish_average(it):
        for dy in range(ny):
            for h in range(HALVES):
                for dc in range(1, nc):
                    csrc = cmod(-dc)
                    recv(
                        av.at[it, ymod(-dy) * nc + csrc, halves[h]],
                        vgc_s.at[it, dy, dc, h], vgc_r.at[it, dy, dc, h], at_view(yy, csrc),
                    )

    far = nz - 2
    ns = jax.named_scope
    with ns("q_load"):
        for p in list(ends[cut:]) + list(range(cut)):
            ag_own(0, p)
        for c in range(nchunk):
            if c + 1 < nchunk:
                load(c + 1).start()
            load(c).wait()
            for b in range(nrow):
                hi, lo = split(fbuf[c % 2, :, b * shard:(b + 1) * shard])
                fhi[b, c * chunk:(c + 1) * chunk] = hi
                flo[b, c * chunk:(c + 1) * chunk] = lo
            if nchunk - c == cut + 1:
                ag_crossed(0)
            if nchunk - c <= cut:
                ag_event(0, 0, cut - nchunk + c)
    with ns("q_ag0"):
        ag_run(0, True)
    with ns("q_res"):
        for c in range(local // sub):
            rows = slice(c * sub, (c + 1) * sub)
            put_rt(rows, y[rows] - s_ref[rows])
    with ns("q_rs0c"):
        rs_compute(0)
    with ns("q_rs0e"):
        @pl.loop(0, nz - 1)
        def _(i):
            rs_event(0, far - i)
        rs_cross(0)
        for p in ends:
            rows = crows if p == cut else rows_of[p]
            wf[1, row, rows] = wf[0, row, rows] - step_size * rs_own(0, p)
            ag_own(1, p)
    with ns("q_fl"):
        ag_flush(0)
        rs_flush(0)
    with ns("q_ag1"):
        ag_run(1, False)
    with ns("q_vsend"):
        view_send(0)
        for c in range(local // sub):
            rows = slice(c * sub, (c + 1) * sub)
            put_rt(rows, y[rows])
        rs_first(1, 0)
    with ns("q_vmid"):
        view_mid(0)
    with ns("q_rs1c"):
        rs_compute(1, 1)
    with ns("q_rs1e"):
        rs_event(1, far)
    with ns("q_vend"):
        for h in range(HALVES):
            view_end(0, h)
    with ns("q_g1"):
        gram_start(0)
    with ns("q_rs1e"):
        @pl.loop(1, nz - 1)
        def _(i):
            rs_event(1, far - i)
    with ns("q_fa"):
        for h in range(HALVES - 1):
            forward_average(0, h)
    with ns("q_g2"):
        gram_views(0)
    with ns("q_fa"):
        forward_average(0, HALVES - 1)
    with ns("q_g3"):
        gram_rows(0)
    with ns("q_fin"):
        rs_cross(1)
        finish_average(0)
        ag_flush(1)
        for v in range(nview):
            put_rt(slice(v * part, (v + 1) * part), av[0, v])
    with ns("q_rs2c"):
        rs_compute(2)
    with ns("q_rs1o"):
        for p in ends:
            rs_own(1, p)
    with ns("q_rs2e"):
        rs_event(2, far)
    with ns("q_nw"):
        steps = gram_end(0)
        next(steps)
        root, frob = next(steps)
    with ns("q_rs2e"):
        for i in range(1, nz - 1):
            rs_event(2, far - i)
            root, frob = next(steps, (root, frob))
        for root, frob in steps:
            pass
        rs_cross(2)
        rootc = split(root.T)
        scale = jnp.sqrt(total / frob)
        for p in ends:
            rs_own(2, p)
    with ns("q_w2"):
        moved = dot3s(rootc, split(zs[0, z])) * scale
        wf[0, row] = wf[1, row] - step_size * (zs[1, z] - moved)
        for p in ends:
            ag_own(2, p)
        flush()
        rs_flush(1)
        rs_flush(2)
    with ns("q_ag2"):
        ag_run(2, False)
    with ns("q_vmid"):
        view_send(1)
        view_mid(1)
        wo_ref[0] = wf[0, row].T
    with ns("q_vend"):
        for h in range(HALVES):
            view_end(1, h)
    with ns("q_g1"):
        gram_start(1)
        gram_views(1)
    with ns("q_g3"):
        gram_rows(1)
        ag_flush(2)
        for h in range(HALVES):
            forward_average(1, h)
    with ns("q_g4"):
        steps = gram_end(1)
    with ns("q_nw"):
        for root, frob in steps:
            pass
        scale = jnp.sqrt(total / frob)
    with ns("q_fina"):
        finish_average(1)
    with ns("q_out"):
        rs = split(root)
        for v in range(nview):
            so_ref[v * part:(v + 1) * part] = dot3s(split(av[1, v]), rs) * scale
        flush()


def solution(mesh):
    nrow, nview = mesh.shape["row"], mesh.shape["view"]
    nx = max(d for d in range(1, math.isqrt(nrow) + 1) if nrow % d == 0)
    nz = nrow // nx
    nc = CORES if nview % CORES == 0 else 1
    ny = nview // nc

    def local(features, view_maps, shared):
        rows, width = features.shape[1], features.shape[2]
        shard, keys = view_maps.shape[1], view_maps.shape[2]
        part, gpart = rows // nview, keys // nrow
        tiles = keys // SUBLANES
        late = tiles * LATE // 32
        sizes = [(tiles - late + CUT - 1 - p) // CUT * SUBLANES for p in range(CUT)]
        pieces = [(sum(sizes[:p]), sizes[p]) for p in range(CUT)]
        cross = (sum(sizes), keys - sum(sizes))
        cut = CUT
        chunk = 256
        dma = pltpu.SemaphoreType.DMA
        sems = []
        for shape in [
            (3, nz + 1, cut + nx), (3, nz, nx, cut + 1), (3, nz, nx, cut), (3, nz + 1, cut),
            (3, nz + 1, nx), (3, nx),
            (ITERS, ny, nc, HALVES), (ITERS, ny, HALVES), (ITERS, ny, HALVES),
            (ITERS, ny, nc, HALVES),
            (ITERS, nrow), (ITERS, nview), (ITERS, nrow),
        ]:
            sems += [dma(shape), dma(shape)]
        vmem = pl.BlockSpec(memory_space=pltpu.VMEM)
        return pl.pallas_call(
            functools.partial(kernel, (nz, nx, ny, nc), pieces, cross),
            out_shape=(
                jax.ShapeDtypeStruct(view_maps.shape, F32),
                jax.ShapeDtypeStruct(shared.shape, F32),
            ),
            in_specs=[pl.BlockSpec(memory_space=pl.ANY), vmem, vmem],
            out_specs=(vmem, vmem),
            scratch_shapes=[
                pltpu.VMEM((nrow, rows, shard), BF16),
                pltpu.VMEM((nrow, rows, shard), BF16),
                pltpu.VMEM((2, chunk, width), F32),
                pltpu.VMEM((keys, rows), BF16),
                pltpu.VMEM((keys, rows), BF16),
                pltpu.VMEM((rows, keys), F32),
                pltpu.VMEM((2, nrow, keys, shard), F32),
                pltpu.VMEM((2, nz, nx - 1, keys, shard), F32),
                pltpu.VMEM((2, nz, nx - 1, keys, shard), F32),
                pltpu.VMEM((2, nz, keys, shard), F32),
                pltpu.VMEM((2, nz + 1, keys, shard), F32),
                pltpu.VMEM((2, nx - 1, max(cross[1], 8), shard), F32),
                pltpu.VMEM((2, nz + 1, nx, max(cross[1], 8), shard), F32),
                pltpu.VMEM((ITERS, ny, part, keys), F32),
                pltpu.VMEM((ITERS, ny, nc - 1, part, keys), F32),
                pltpu.VMEM((ITERS, ny, part, keys), F32),
                pltpu.VMEM((ITERS, nview, part, keys), F32),
                pltpu.VMEM((ITERS, nrow, gpart, keys), F32),
                pltpu.VMEM((ITERS, nrow, gpart, keys), F32),
                pltpu.VMEM((ITERS, nview, gpart, keys), F32),
                pltpu.VMEM((ITERS, nrow, gpart, keys), F32),
                dma((2,)),
            ] + sems,
            compiler_params=pltpu.CompilerParams(
                collective_id=0, has_side_effects=True, vmem_limit_bytes=67043328
            ),
        )(features, view_maps, shared)

    in_specs = (P("view", "row", None), P("view", "row", None), P("row", None))
    out_specs = (P("view", "row", None), P("row", None))
    return jax.shard_map(local, mesh=mesh, in_specs=in_specs, out_specs=out_specs, check_vma=False)
```

```python
import functools
import math

import jax
import jax.numpy as jnp
from jax import lax
from jax.experimental import pallas as pl
from jax.experimental.pallas import tpu as pltpu
from jax.sharding import PartitionSpec as P

ITERS = 2
NEWTON = 5
STEP_RATE = 0.5
CORES = 2
HALVES = 2
CUT = 2
MESH = pl.DeviceIdType.MESH
F32 = jnp.float32
BF16 = jnp.bfloat16


def split(x):
    hi = x.astype(BF16)
    return hi, (x - hi.astype(F32)).astype(BF16)


def dot3s(a, b):
    lhs = jnp.concatenate([a[0], a[1], a[0]], axis=1)
    rhs = jnp.concatenate([b[0], b[0], b[1]], axis=0)
    return jnp.dot(lhs, rhs, preferred_element_type=F32)


def dot3(a, b):
    return dot3s(split(a), split(b))


def newton_steps(gram):
    size = gram.shape[0]
    frob = jnp.sqrt(jnp.sum(gram * gram, keepdims=True))
    scaled = gram / frob
    rows = lax.broadcasted_iota(jnp.int32, (size, size), 0)
    cols = lax.broadcasted_iota(jnp.int32, (size, size), 1)
    eye = jnp.where(rows == cols, 1.0, 0.0).astype(F32)
    root = None
    for step in range(NEWTON):
        ym = split(scaled)
        zy = scaled if root is None else dot3s(split(root), ym)
        corr = 1.5 * eye - 0.5 * zy
        cs = split(corr)
        if step < NEWTON - 1:
            scaled = dot3s(ym, cs)
        root = corr if root is None else dot3s(cs, split(root))
        yield root, frob


def kernel(
    dims, pieces,
    f_ref, w_ref, s_hbm, wo_ref, ao_hbm, root_ref,
    s_ref, fhi, flo, fbuf, rthi, rtlo, y, wf, xs, xr, zs, zr,
    vs, cr, yr, av, gram, gr, gv, gfull,
    f_sem, s_sem, o_sem, agz_s, agz_r, agx_s, agx_r, rsx_s, rsx_r, rsz_s, rsz_r,
    vrc_s, vrc_r, vry_s, vry_r, vgy_s, vgy_r, vgc_s, vgc_r,
    g1_s, g1_r, g2_s, g2_r, g3_s, g3_r,
):
    nz, nx, ny, nc = dims
    nrow, nview = nz * nx, ny * nc
    row, view = lax.axis_index("row"), lax.axis_index("view")
    z, x = row // nx, row % nx
    yy, core = view // nc, view % nc
    local = y.shape[0]
    width = f_ref.shape[2]
    keys = y.shape[1]
    shard = w_ref.shape[1]
    total = local * nrow
    step_size = STEP_RATE * width / total
    chunk = fbuf.shape[1]
    nchunk = local // chunk
    part = local // nview
    gpart = keys // nrow
    cut = len(pieces)
    rows_of = [pl.ds(a, n) for a, n in pieces]
    sub = 512

    def at_row(zz, xx):
        return {"row": zz * nx + xx}

    def at_view(y1, c1):
        return {"view": y1 * nc + c1}

    def xmod(d):
        return lax.rem(x + d + nx, nx)

    def ymod(d):
        return lax.rem(yy + d + ny, ny)

    def cmod(d):
        return lax.rem(core + d + nc, nc)

    pending = []

    def remote(src, dst, ssem, rsem, dev):
        return pltpu.make_async_remote_copy(
            src_ref=src, dst_ref=dst, send_sem=ssem, recv_sem=rsem,
            device_id=dev, device_id_type=MESH,
        )

    def send(src, dst, ssem, rsem, dev):
        copy = remote(src, dst, ssem, rsem, dev)
        copy.start()
        pending.append(copy)

    def recv(buf, ssem, rsem, dev):
        remote(buf, buf, ssem, rsem, dev).wait_recv()

    def flush():
        for copy in pending:
            copy.wait_send()
        pending.clear()

    def line(j):
        low, high = z, nz - 1 - z
        m = jnp.minimum(low, high)
        near = j < 2 * m
        k = jnp.where(near, j // 2 + 1, j - m + 1)
        far_d = jnp.where(low > high, 1, -1)
        d = jnp.where(near, 1 - 2 * (j % 2), far_d)
        return z - d * k, d

    def inside(zz):
        return jnp.logical_and(zz >= 0, zz < nz)

    def load(c):
        return pltpu.make_async_copy(
            f_ref.at[0, pl.ds(c * chunk, chunk)], fbuf.at[c % 2], f_sem.at[c % 2]
        )

    load(0).start()
    shared_load = pltpu.make_async_copy(s_hbm, s_ref, s_sem)
    wf[0, row] = w_ref[0].T
    barrier = pltpu.get_barrier_semaphore()
    for d in range(1, nrow):
        pl.semaphore_signal(
            barrier, inc=1, device_id={"row": lax.rem(row + d, nrow)}, device_id_type=MESH
        )
    for d in range(1, nview):
        pl.semaphore_signal(
            barrier, inc=1, device_id={"view": lax.rem(view + d, nview)}, device_id_type=MESH
        )
    pl.semaphore_wait(barrier, nrow + nview - 2)

    def ag_z(g, src, p, slot, to):
        ref = wf.at[g % 2, src * nx + x, rows_of[p]]
        return remote(ref, ref, agz_s.at[slot, p], agz_r.at[src, p], at_row(to, x))

    def ag_x(g, src, dx, p):
        ref = wf.at[g % 2, src * nx + x, rows_of[p]]
        return remote(
            ref, ref, agx_s.at[src, dx - 1, p], agx_r.at[src, dx - 1, p], at_row(z, xmod(dx))
        )

    def ag_both(g, p, wait=False):
        @pl.when(z + 1 < nz)
        def _():
            copy = ag_z(g, z, p, z, z + 1)
            copy.wait_send() if wait else copy.start()

        @pl.when(z > 0)
        def _():
            copy = ag_z(g, z, p, nz, z - 1)
            copy.wait_send() if wait else copy.start()

    def ag_own(g, p):
        ag_both(g, p)
        for dx in range(1, nx):
            ag_x(g, z, dx, p).start()

    def ag_relay(g, j, p, wait=False):
        src, d = line(j)
        if not wait:
            ag_z(g, src, p, src, z - d).wait_recv()

        @pl.when(inside(z + d))
        def _():
            copy = ag_z(g, src, p, src, z + d)
            copy.wait_send() if wait else copy.start()

    def ag_event(g, j, p):
        ag_relay(g, j, p)
        for dx in range(1, nx):
            ag_x(g, line(j)[0], dx, p).start()

    def ag_last(g, src):
        for dx in range(1, nx):
            block = src * nx + xmod(-dx)
            for p in range(cut):
                recv(
                    wf.at[g % 2, block, rows_of[p]],
                    agx_s.at[src, dx - 1, p], agx_r.at[src, dx - 1, p], at_row(z, xmod(-dx)),
                )
            project(g, block, False)

    def ag_flush(g):
        for p in range(cut):
            ag_both(g, p, True)
            for dx in range(1, nx):
                ag_x(g, z, dx, p).wait_send()

        @pl.loop(0, nz - 1)
        def _(j):
            for p in range(cut):
                ag_relay(g, j, p, True)
                for dx in range(1, nx):
                    ag_x(g, line(j)[0], dx, p).wait_send()

    def project(g, block, first):
        hi, lo = split(wf[g % 2, block])
        rhs = jnp.concatenate([hi, hi, lo], axis=1)

        @pl.loop(0, local // sub)
        def _(c):
            rows = pl.ds(pl.multiple_of(c * sub, sub), sub)
            fh, fl = fhi[block, rows], flo[block, rows]
            out = lax.dot_general(
                jnp.concatenate([fh, fl, fh], axis=1), rhs, (((1,), (1,)), ((), ())),
                preferred_element_type=F32,
            )
            if first:
                y[rows] = out
            else:
                y[rows] += out

    def ag_run(g, started):
        project(g, row, True)
        if not started:
            for p in range(cut):
                ag_event(g, 0, p)

        @pl.loop(0, nz - 1)
        def _(j):
            @pl.when(j + 1 < nz - 1)
            def _():
                for p in range(cut):
                    ag_event(g, j + 1, p)

            project(g, line(j)[0] * nx + x, False)
            ag_last(g, jnp.where(j == 0, z, line(j - 1)[0]))

        ag_last(g, line(nz - 2)[0])

    def put_rt(rows, value):
        hi, lo = split(value.T)
        rthi[:, rows] = hi
        rtlo[:, rows] = lo

    def gradient(block):
        hi, lo = fhi[block], flo[block]
        rh = rthi[...]
        out = jnp.dot(rh, hi, preferred_element_type=F32)
        out += jnp.dot(rh, lo, preferred_element_type=F32)
        out += jnp.dot(rtlo[...], hi, preferred_element_type=F32)
        return out

    def order(i):
        return jnp.where(i == nz - 1, z, line(nz - 2 - i)[0])

    def rs_x(r, t, dx, p):
        return remote(
            xs.at[r % 2, t, dx - 1, rows_of[p]], xr.at[r % 2, t, dx - 1, rows_of[p]],
            rsx_s.at[r % 2, t, dx - 1, p], rsx_r.at[r % 2, t, dx - 1, p], at_row(z, xmod(dx)),
        )

    def slot_of(t, d):
        return jnp.where(jnp.logical_and(d < 0, t == z - d), nz, t)

    def rs_z(r, t, d, p):
        slot = slot_of(t, d)
        return remote(
            zs.at[r % 2, t, rows_of[p]], zr.at[r % 2, slot, rows_of[p]],
            rsz_s.at[r % 2, t, p], rsz_r.at[r % 2, slot, p], at_row(z - d, x),
        )

    def rs_first(r, i):
        t = order(i)
        for dx in range(1, nx):
            xs[r % 2, t, dx - 1] = gradient(t * nx + xmod(dx))
            for p in range(cut):
                rs_x(r, t, dx, p).start()

    def rs_compute(r, begun=0):
        @pl.loop(begun, nz)
        def _(i):
            rs_first(r, i)

        @pl.loop(0, nz)
        def _(i):
            t = order(i)
            zs[r % 2, t] = gradient(t * nx + x)

    def rs_over_x(r, t, p):
        acc = zs[r % 2, t, rows_of[p]]
        for dx in range(1, nx):
            recv(
                xr.at[r % 2, t, dx - 1, rows_of[p]],
                rsx_s.at[r % 2, t, dx - 1, p], rsx_r.at[r % 2, t, dx - 1, p], at_row(z, xmod(-dx)),
            )
            acc = acc + xr[r % 2, t, dx - 1, rows_of[p]]
        return acc

    def rs_take(r, t, slot, p, frm):
        recv(
            zr.at[r % 2, slot, rows_of[p]], rsz_s.at[r % 2, t, p], rsz_r.at[r % 2, slot, p],
            at_row(frm, x),
        )
        zs[r % 2, t, rows_of[p]] += zr[r % 2, slot, rows_of[p]]

    def rs_event(r, j):
        t, d = line(j)
        for p in range(cut):
            zs[r % 2, t, rows_of[p]] = rs_over_x(r, t, p)

            @pl.when(inside(z + d))
            def _():
                rs_take(r, t, t, p, z + d)

            rs_z(r, t, d, p).start()

    def rs_own(r, p):
        zs[r % 2, z, rows_of[p]] = rs_over_x(r, z, p)

        @pl.when(z + 1 < nz)
        def _():
            rs_take(r, z, z, p, z + 1)

        @pl.when(z > 0)
        def _():
            rs_take(r, z, nz, p, z - 1)

        return zs[r % 2, z, rows_of[p]]

    def rs_flush(r):
        @pl.loop(0, nz)
        def _(i):
            t = order(i)
            for dx in range(1, nx):
                for p in range(cut):
                    rs_x(r, t, dx, p).wait_send()

        @pl.loop(0, nz - 1)
        def _(j):
            t, d = line(j)
            for p in range(cut):
                rs_z(r, t, d, p).wait_send()

    half = part // HALVES
    halves = [pl.ds(h * half, half) for h in range(HALVES)]

    def yblock(block, h):
        return pl.ds(pl.multiple_of(block * part + h * half, half), half)

    def view_send(it):
        for dy in list(range(1, ny)) + [0]:
            for h in range(HALVES):
                for dc in range(1, nc):
                    ct = cmod(dc)
                    send(
                        y.at[yblock(ymod(dy) * nc + ct, h)], cr.at[it, dy, dc - 1, halves[h]],
                        vrc_s.at[dy, dc - 1, h], vrc_r.at[dy, dc - 1, h], at_view(yy, ct),
                    )

    def view_mid(it):
        for dy in list(range(1, ny)) + [0]:
            for h in range(HALVES):
                acc = y[yblock(ymod(dy) * nc + core, h)]
                for dc in range(1, nc):
                    recv(
                        cr.at[it, dy, dc - 1, halves[h]],
                        vrc_s.at[dy, dc - 1, h], vrc_r.at[dy, dc - 1, h],
                        at_view(yy, cmod(-dc)),
                    )
                    acc = acc + cr[it, dy, dc - 1, halves[h]]
                vs[it, dy, halves[h]] = acc
                if dy:
                    send(
                        vs.at[it, dy, halves[h]], yr.at[it, dy, halves[h]],
                        vry_s.at[dy - 1, h], vry_r.at[dy - 1, h], at_view(ymod(dy), core),
                    )

    def view_end(it, h):
        acc = vs[it, 0, halves[h]]
        for dy in range(1, ny):
            recv(
                yr.at[it, dy, halves[h]], vry_s.at[dy - 1, h], vry_r.at[dy - 1, h],
                at_view(ymod(-dy), core),
            )
            acc = acc + yr[it, dy, halves[h]]
        av[it, view, halves[h]] = acc / nview
        own = av.at[it, view, halves[h]]
        for dy in range(1, ny):
            send(
                own, own, vgy_s.at[dy - 1, h], vgy_r.at[dy - 1, h], at_view(ymod(dy), core)
            )
        for dc in range(1, nc):
            send(
                own, own, vgc_s.at[0, dc - 1, h], vgc_r.at[0, dc - 1, h],
                at_view(yy, cmod(dc)),
            )

    def gram_start(it):
        own = av[it, view]
        hi, lo = split(own)
        thi, tlo = split(own.T)
        gram[it] = dot3s((thi, tlo), (hi, lo)).reshape(nrow, gpart, keys)
        for d in range(1, nrow):
            to = lax.rem(row + d, nrow)
            send(
                gram.at[it, to], gr.at[it, d], g1_s.at[d - 1], g1_r.at[d - 1], {"row": to}
            )

    def gram_views(it):
        acc = gram[it, row]
        for d in range(1, nrow):
            recv(
                gr.at[it, d], g1_s.at[d - 1], g1_r.at[d - 1],
                {"row": lax.rem(row - d + nrow, nrow)},
            )
            acc = acc + gr[it, d]
        gv[it, 0] = acc
        for d in range(1, nview):
            send(
                gv.at[it, 0], gv.at[it, d], g2_s.at[d - 1], g2_r.at[d - 1],
                {"view": lax.rem(view + d, nview)},
            )

    def gram_rows(it):
        acc = gv[it, 0]
        for d in range(1, nview):
            recv(
                gv.at[it, d], g2_s.at[d - 1], g2_r.at[d - 1],
                {"view": lax.rem(view - d + nview, nview)},
            )
            acc = acc + gv[it, d]
        gfull[it, row] = acc
        mine = gfull.at[it, row]
        for d in range(1, nrow):
            send(
                mine, mine, g3_s.at[d - 1], g3_r.at[d - 1],
                {"row": lax.rem(row + d, nrow)},
            )

    def gram_end(it):
        for d in range(1, nrow):
            src = lax.rem(row - d + nrow, nrow)
            recv(gfull.at[it, src], g3_s.at[d - 1], g3_r.at[d - 1], {"row": src})
        return newton_steps(gfull[it].reshape(keys, keys))

    def forward_average(it, h):
        for dy in range(1, ny):
            ysrc = ymod(-dy)
            got = av.at[it, ysrc * nc + core, halves[h]]
            recv(got, vgy_s.at[dy - 1, h], vgy_r.at[dy - 1, h], at_view(ysrc, core))
            for dc in range(1, nc):
                send(
                    got, got, vgc_s.at[dy, dc - 1, h], vgc_r.at[dy, dc - 1, h],
                    at_view(yy, cmod(dc)),
                )

    def finish_average(it):
        for dy in range(ny):
            for h in range(HALVES):
                for dc in range(1, nc):
                    csrc = cmod(-dc)
                    recv(
                        av.at[it, ymod(-dy) * nc + csrc, halves[h]],
                        vgc_s.at[dy, dc - 1, h], vgc_r.at[dy, dc - 1, h], at_view(yy, csrc),
                    )

    far = nz - 2
    ns = jax.named_scope
    with ns("q_load"):
        for p in range(cut):
            ag_own(0, p)
        for c in range(nchunk):
            if c + 1 < nchunk:
                load(c + 1).start()
            else:
                shared_load.start()
            load(c).wait()
            for b in range(nrow):
                hi, lo = split(fbuf[c % 2, :, b * shard:(b + 1) * shard])
                fhi[b, c * chunk:(c + 1) * chunk] = hi
                flo[b, c * chunk:(c + 1) * chunk] = lo
            if nchunk - c <= cut:
                ag_event(0, 0, cut - nchunk + c)
    with ns("q_ag0"):
        ag_run(0, True)
    with ns("q_res"):
        shared_load.wait()
        for c in range(local // sub):
            rows = slice(c * sub, (c + 1) * sub)
            put_rt(rows, y[rows] - s_ref[rows])
    with ns("q_rs0c"):
        rs_compute(0)
    with ns("q_rs0e"):
        @pl.loop(0, nz - 1)
        def _(i):
            rs_event(0, far - i)
        ag_flush(0)
        for p in range(cut):
            rows = rows_of[p]
            wf[1, row, rows] = wf[0, row, rows] - step_size * rs_own(0, p)
            ag_own(1, p)
    with ns("q_fl"):
        rs_flush(0)
    with ns("q_ag1"):
        ag_run(1, False)
    with ns("q_vsend"):
        view_send(0)
        for c in range(local // sub):
            rows = slice(c * sub, (c + 1) * sub)
            put_rt(rows, y[rows])
        rs_first(1, 0)
    with ns("q_vmid"):
        view_mid(0)
    with ns("q_rs1c"):
        rs_compute(1, 1)
    with ns("q_rs1e"):
        rs_event(1, far)
    with ns("q_vend"):
        for h in range(HALVES):
            view_end(0, h)
    with ns("q_g1"):
        gram_start(0)
    with ns("q_rs1e"):
        @pl.loop(1, nz - 1)
        def _(i):
            rs_event(1, far - i)
    with ns("q_fa"):
        for h in range(HALVES - 1):
            forward_average(0, h)
    with ns("q_g2"):
        gram_views(0)
    with ns("q_fa"):
        forward_average(0, HALVES - 1)
    with ns("q_g3"):
        gram_rows(0)
    with ns("q_fin"):
        finish_average(0)
        ag_flush(1)
        for v in range(nview):
            put_rt(slice(v * part, (v + 1) * part), av[0, v])
    with ns("q_rs2c"):
        rs_compute(2)
    with ns("q_rs1o"):
        for p in range(cut):
            rs_own(1, p)
    with ns("q_rs2e"):
        rs_event(2, far)
    with ns("q_nw"):
        steps = gram_end(0)
        next(steps)
        root, frob = next(steps)
    with ns("q_rs2e"):
        for i in range(1, nz - 1):
            rs_event(2, far - i)
            root, frob = next(steps, (root, frob))
        for root, frob in steps:
            pass
        rootc = split(root.T)
        scale = jnp.sqrt(total / frob)
        for p in range(cut):
            rs_own(2, p)
    with ns("q_w2"):
        moved = dot3s(rootc, split(zs[0, z])) * scale
        wf[0, row] = wf[1, row] - step_size * (zs[1, z] - moved)
        for p in range(cut):
            ag_own(2, p)
        flush()
        rs_flush(1)
        rs_flush(2)
    with ns("q_ag2"):
        ag_run(2, False)
    with ns("q_vmid"):
        view_send(1)
        view_mid(1)
        wo_ref[0] = wf[0, row].T
    with ns("q_vend"):
        for h in range(HALVES):
            view_end(1, h)
    with ns("q_g1"):
        gram_start(1)
        gram_views(1)
    with ns("q_g3"):
        gram_rows(1)
        ag_flush(2)
        for h in range(HALVES):
            forward_average(1, h)
        finish_average(1)
        out = pltpu.make_async_copy(av.at[1], ao_hbm, o_sem)
        out.start()
    with ns("q_g4"):
        steps = gram_end(1)
    with ns("q_nw"):
        for root, frob in steps:
            pass
        root_ref[...] = root * jnp.sqrt(total / frob)
    with ns("q_out"):
        out.wait()
        flush()


def last_product(w_ref, a_ref, root_ref, wo_ref, so_ref):
    @pl.when(pl.program_id(0) == 0)
    def _():
        wo_ref[...] = w_ref[...]

    so_ref[...] = dot3(a_ref[...], root_ref[...])


def solution(mesh):
    nrow, nview = mesh.shape["row"], mesh.shape["view"]
    nx = max(d for d in range(1, math.isqrt(nrow) + 1) if nrow % d == 0)
    nz = nrow // nx
    nc = CORES if nview % CORES == 0 else 1
    ny = nview // nc

    def local(features, view_maps, shared):
        rows, width = features.shape[1], features.shape[2]
        shard, keys = view_maps.shape[1], view_maps.shape[2]
        part, gpart = rows // nview, keys // nrow
        cut = CUT
        pieces = [(p * keys // cut, keys // cut) for p in range(cut)]
        chunk = 256
        dma = pltpu.SemaphoreType.DMA
        sems = []
        for shape in [
            (nz + 1, cut), (nz, nx - 1, cut), (2, nz, nx - 1, cut), (2, nz + 1, cut),
            (ny, nc - 1, HALVES), (ny - 1, HALVES), (ny - 1, HALVES), (ny, nc - 1, HALVES),
            (nrow - 1,), (nview - 1,), (nrow - 1,),
        ]:
            sems += [dma(shape), dma(shape)]
        vmem = pl.BlockSpec(memory_space=pltpu.VMEM)
        hbm = pl.BlockSpec(memory_space=pl.ANY)
        maps, average, root = pl.pallas_call(
            functools.partial(kernel, (nz, nx, ny, nc), pieces),
            out_shape=(
                jax.ShapeDtypeStruct(view_maps.shape, F32),
                jax.ShapeDtypeStruct((nview, part, keys), F32),
                jax.ShapeDtypeStruct((keys, keys), F32),
            ),
            in_specs=[hbm, vmem, hbm],
            out_specs=(vmem, hbm, vmem),
            scratch_shapes=[
                pltpu.VMEM((rows, keys), F32),
                pltpu.VMEM((nrow, rows, shard), BF16),
                pltpu.VMEM((nrow, rows, shard), BF16),
                pltpu.VMEM((2, chunk, width), F32),
                pltpu.VMEM((keys, rows), BF16),
                pltpu.VMEM((keys, rows), BF16),
                pltpu.VMEM((rows, keys), F32),
                pltpu.VMEM((2, nrow, keys, shard), F32),
                pltpu.VMEM((2, nz, nx - 1, keys, shard), F32),
                pltpu.VMEM((2, nz, nx - 1, keys, shard), F32),
                pltpu.VMEM((2, nz, keys, shard), F32),
                pltpu.VMEM((2, nz + 1, keys, shard), F32),
                pltpu.VMEM((ITERS, ny, part, keys), F32),
                pltpu.VMEM((ITERS, ny, nc - 1, part, keys), F32),
                pltpu.VMEM((ITERS, ny, part, keys), F32),
                pltpu.VMEM((ITERS, nview, part, keys), F32),
                pltpu.VMEM((ITERS, nrow, gpart, keys), F32),
                pltpu.VMEM((ITERS, nrow, gpart, keys), F32),
                pltpu.VMEM((ITERS, nview, gpart, keys), F32),
                pltpu.VMEM((ITERS, nrow, gpart, keys), F32),
                dma((2,)), dma, dma,
            ] + sems,
            compiler_params=pltpu.CompilerParams(
                collective_id=0, has_side_effects=True, vmem_limit_bytes=67043328
            ),
        )(features, view_maps, shared)
        whole = pl.BlockSpec((1, shard, keys), lambda c: (0, 0, 0))
        tile = pl.BlockSpec((part, keys), lambda c: (c, 0))
        return pl.pallas_call(
            last_product,
            grid=(nview,),
            out_shape=(
                jax.ShapeDtypeStruct(view_maps.shape, F32),
                jax.ShapeDtypeStruct(shared.shape, F32),
            ),
            in_specs=[whole, tile, pl.BlockSpec((keys, keys), lambda c: (0, 0))],
            out_specs=(whole, tile),
        )(maps, average.reshape(rows, keys), root)

    in_specs = (P("view", "row", None), P("view", "row", None), P("row", None))
    out_specs = (P("view", "row", None), P("row", None))
    return jax.shard_map(local, mesh=mesh, in_specs=in_specs, out_specs=out_specs, check_vma=False)
```

```python
import functools
import math

import jax
import jax.numpy as jnp
from jax import lax
from jax.experimental import pallas as pl
from jax.experimental.pallas import tpu as pltpu
from jax.sharding import PartitionSpec as P

ITERS = 2
NEWTON = 5
STEP_RATE = 0.5
CORES = 2
HALVES = 2
CUT = 2
LAST = 2
MESH = pl.DeviceIdType.MESH
F32 = jnp.float32
BF16 = jnp.bfloat16


def split(x):
    hi = x.astype(BF16)
    return hi, (x - hi.astype(F32)).astype(BF16)


def dot3s(a, b):
    lhs = jnp.concatenate([a[0], a[1], a[0]], axis=1)
    rhs = jnp.concatenate([b[0], b[0], b[1]], axis=0)
    return jnp.dot(lhs, rhs, preferred_element_type=F32)


def dot3(a, b):
    return dot3s(split(a), split(b))


def newton_steps(gram):
    size = gram.shape[0]
    frob = jnp.sqrt(jnp.sum(gram * gram, keepdims=True))
    scaled = gram / frob
    rows = lax.broadcasted_iota(jnp.int32, (size, size), 0)
    cols = lax.broadcasted_iota(jnp.int32, (size, size), 1)
    eye = jnp.where(rows == cols, 1.0, 0.0).astype(F32)
    root = None
    for step in range(NEWTON):
        ym = split(scaled)
        zy = scaled if root is None else dot3s(split(root), ym)
        corr = 1.5 * eye - 0.5 * zy
        cs = split(corr)
        if step < NEWTON - 1:
            scaled = dot3s(ym, cs)
        root = corr if root is None else dot3s(cs, split(root))
        yield root, frob


def kernel(
    dims, pieces,
    f_ref, w_ref, s_hbm, wo_ref, ao_hbm, root_ref,
    s_ref, fhi, flo, fbuf, rthi, rtlo, y, wf, xs, xr, zs, zr,
    vs, cr, yr, av, gram, gr, gv, gfull,
    f_sem, s_sem, o_sem, agz_s, agz_r, agx_s, agx_r, rsx_s, rsx_r, rsz_s, rsz_r,
    vrc_s, vrc_r, vry_s, vry_r, vgy_s, vgy_r, vgc_s, vgc_r,
    g1_s, g1_r, g2_s, g2_r, g3_s, g3_r,
):
    nz, nx, ny, nc = dims
    nrow, nview = nz * nx, ny * nc
    row, view = lax.axis_index("row"), lax.axis_index("view")
    z, x = row // nx, row % nx
    yy, core = view // nc, view % nc
    local = y.shape[0]
    width = f_ref.shape[2]
    keys = y.shape[1]
    shard = w_ref.shape[1]
    total = local * nrow
    step_size = STEP_RATE * width / total
    chunk = fbuf.shape[1]
    nchunk = local // chunk
    part = local // nview
    side = keys // 2
    gpart = side // nrow
    cut = len(pieces)
    rows_of = [pl.ds(a, n) for a, n in pieces]
    sub = 512

    def at_row(zz, xx):
        return {"row": zz * nx + xx}

    def at_view(y1, c1):
        return {"view": y1 * nc + c1}

    def xmod(d):
        return lax.rem(x + d + nx, nx)

    def ymod(d):
        return lax.rem(yy + d + ny, ny)

    def cmod(d):
        return lax.rem(core + d + nc, nc)

    pending = []

    def remote(src, dst, ssem, rsem, dev):
        return pltpu.make_async_remote_copy(
            src_ref=src, dst_ref=dst, send_sem=ssem, recv_sem=rsem,
            device_id=dev, device_id_type=MESH,
        )

    def send(src, dst, ssem, rsem, dev):
        copy = remote(src, dst, ssem, rsem, dev)
        copy.start()
        pending.append(copy)

    def recv(buf, ssem, rsem, dev):
        remote(buf, buf, ssem, rsem, dev).wait_recv()

    def flush():
        for copy in pending:
            copy.wait_send()
        pending.clear()

    def line(j):
        low, high = z, nz - 1 - z
        m = jnp.minimum(low, high)
        near = j < 2 * m
        k = jnp.where(near, j // 2 + 1, j - m + 1)
        far_d = jnp.where(low > high, 1, -1)
        d = jnp.where(near, 1 - 2 * (j % 2), far_d)
        return z - d * k, d

    def inside(zz):
        return jnp.logical_and(zz >= 0, zz < nz)

    def load(c):
        return pltpu.make_async_copy(
            f_ref.at[0, pl.ds(c * chunk, chunk)], fbuf.at[c % 2], f_sem.at[c % 2]
        )

    load(0).start()
    shared_load = pltpu.make_async_copy(s_hbm, s_ref, s_sem)
    wf[0, row] = w_ref[0].T
    barrier = pltpu.get_barrier_semaphore()
    for d in range(1, nrow):
        pl.semaphore_signal(
            barrier, inc=1, device_id={"row": lax.rem(row + d, nrow)}, device_id_type=MESH
        )
    for d in range(1, nview):
        pl.semaphore_signal(
            barrier, inc=1, device_id={"view": lax.rem(view + d, nview)}, device_id_type=MESH
        )
    pl.semaphore_wait(barrier, nrow + nview - 2)

    def ag_z(g, src, p, slot, to):
        ref = wf.at[g % 2, src * nx + x, rows_of[p]]
        return remote(ref, ref, agz_s.at[slot, p], agz_r.at[src, p], at_row(to, x))

    def ag_x(g, src, dx, p):
        ref = wf.at[g % 2, src * nx + x, rows_of[p]]
        return remote(
            ref, ref, agx_s.at[src, dx - 1, p], agx_r.at[src, dx - 1, p], at_row(z, xmod(dx))
        )

    def ag_both(g, p, wait=False):
        @pl.when(z + 1 < nz)
        def _():
            copy = ag_z(g, z, p, z, z + 1)
            copy.wait_send() if wait else copy.start()

        @pl.when(z > 0)
        def _():
            copy = ag_z(g, z, p, nz, z - 1)
            copy.wait_send() if wait else copy.start()

    def ag_own(g, p):
        ag_both(g, p)
        for dx in range(1, nx):
            ag_x(g, z, dx, p).start()

    def ag_relay(g, j, p, wait=False):
        src, d = line(j)
        if not wait:
            ag_z(g, src, p, src, z - d).wait_recv()

        @pl.when(inside(z + d))
        def _():
            copy = ag_z(g, src, p, src, z + d)
            copy.wait_send() if wait else copy.start()

    def ag_event(g, j, p):
        ag_relay(g, j, p)
        for dx in range(1, nx):
            ag_x(g, line(j)[0], dx, p).start()

    def ag_last(g, src):
        for dx in range(1, nx):
            block = src * nx + xmod(-dx)
            for p in range(cut):
                recv(
                    wf.at[g % 2, block, rows_of[p]],
                    agx_s.at[src, dx - 1, p], agx_r.at[src, dx - 1, p], at_row(z, xmod(-dx)),
                )
            project(g, block, False)

    def ag_flush(g):
        for p in range(cut):
            ag_both(g, p, True)
            for dx in range(1, nx):
                ag_x(g, z, dx, p).wait_send()

        @pl.loop(0, nz - 1)
        def _(j):
            for p in range(cut):
                ag_relay(g, j, p, True)
                for dx in range(1, nx):
                    ag_x(g, line(j)[0], dx, p).wait_send()

    def project(g, block, first):
        hi, lo = split(wf[g % 2, block])
        rhs = jnp.concatenate([hi, hi, lo], axis=1)

        @pl.loop(0, local // sub)
        def _(c):
            rows = pl.ds(pl.multiple_of(c * sub, sub), sub)
            fh, fl = fhi[block, rows], flo[block, rows]
            out = lax.dot_general(
                jnp.concatenate([fh, fl, fh], axis=1), rhs, (((1,), (1,)), ((), ())),
                preferred_element_type=F32,
            )
            if first:
                y[rows] = out
            else:
                y[rows] += out

    def ag_run(g, started):
        project(g, row, True)
        if not started:
            for p in range(cut):
                ag_event(g, 0, p)

        @pl.loop(0, nz - 1)
        def _(j):
            @pl.when(j + 1 < nz - 1)
            def _():
                for p in range(cut):
                    ag_event(g, j + 1, p)

            project(g, line(j)[0] * nx + x, False)
            ag_last(g, jnp.where(j == 0, z, line(j - 1)[0]))

        ag_last(g, line(nz - 2)[0])

    def put_rt(rows, value):
        hi, lo = split(value.T)
        rthi[:, rows] = hi
        rtlo[:, rows] = lo

    def gradient(block):
        hi, lo = fhi[block], flo[block]
        rh = rthi[...]
        out = jnp.dot(rh, hi, preferred_element_type=F32)
        out += jnp.dot(rh, lo, preferred_element_type=F32)
        out += jnp.dot(rtlo[...], hi, preferred_element_type=F32)
        return out

    def order(i):
        return jnp.where(i == nz - 1, z, line(nz - 2 - i)[0])

    def rs_x(r, t, dx, p):
        return remote(
            xs.at[r % 2, t, dx - 1, rows_of[p]], xr.at[r % 2, t, dx - 1, rows_of[p]],
            rsx_s.at[r % 2, t, dx - 1, p], rsx_r.at[r % 2, t, dx - 1, p], at_row(z, xmod(dx)),
        )

    def slot_of(t, d):
        return jnp.where(jnp.logical_and(d < 0, t == z - d), nz, t)

    def rs_z(r, t, d, p):
        slot = slot_of(t, d)
        return remote(
            zs.at[r % 2, t, rows_of[p]], zr.at[r % 2, slot, rows_of[p]],
            rsz_s.at[r % 2, t, p], rsz_r.at[r % 2, slot, p], at_row(z - d, x),
        )

    def rs_first(r, i):
        t = order(i)
        for dx in range(1, nx):
            xs[r % 2, t, dx - 1] = gradient(t * nx + xmod(dx))
            for p in range(cut):
                rs_x(r, t, dx, p).start()

    def rs_compute(r, begun=0):
        @pl.loop(begun, nz)
        def _(i):
            rs_first(r, i)

        @pl.loop(0, nz)
        def _(i):
            t = order(i)
            zs[r % 2, t] = gradient(t * nx + x)

    def rs_over_x(r, t, p):
        acc = zs[r % 2, t, rows_of[p]]
        for dx in range(1, nx):
            recv(
                xr.at[r % 2, t, dx - 1, rows_of[p]],
                rsx_s.at[r % 2, t, dx - 1, p], rsx_r.at[r % 2, t, dx - 1, p], at_row(z, xmod(-dx)),
            )
            acc = acc + xr[r % 2, t, dx - 1, rows_of[p]]
        return acc

    def rs_take(r, t, slot, p, frm):
        recv(
            zr.at[r % 2, slot, rows_of[p]], rsz_s.at[r % 2, t, p], rsz_r.at[r % 2, slot, p],
            at_row(frm, x),
        )
        zs[r % 2, t, rows_of[p]] += zr[r % 2, slot, rows_of[p]]

    def rs_event(r, j):
        t, d = line(j)
        for p in range(cut):
            zs[r % 2, t, rows_of[p]] = rs_over_x(r, t, p)

            @pl.when(inside(z + d))
            def _():
                rs_take(r, t, t, p, z + d)

            rs_z(r, t, d, p).start()

    def rs_own(r, p):
        zs[r % 2, z, rows_of[p]] = rs_over_x(r, z, p)

        @pl.when(z + 1 < nz)
        def _():
            rs_take(r, z, z, p, z + 1)

        @pl.when(z > 0)
        def _():
            rs_take(r, z, nz, p, z - 1)

        return zs[r % 2, z, rows_of[p]]

    def rs_flush(r):
        @pl.loop(0, nz)
        def _(i):
            t = order(i)
            for dx in range(1, nx):
                for p in range(cut):
                    rs_x(r, t, dx, p).wait_send()

        @pl.loop(0, nz - 1)
        def _(j):
            t, d = line(j)
            for p in range(cut):
                rs_z(r, t, d, p).wait_send()

    half = part // HALVES
    halves = [pl.ds(h * half, half) for h in range(HALVES)]

    def yblock(block, h):
        return pl.ds(pl.multiple_of(block * part + h * half, half), half)

    def view_send(it):
        for dy in list(range(1, ny)) + [0]:
            for h in range(HALVES):
                for dc in range(1, nc):
                    ct = cmod(dc)
                    send(
                        y.at[yblock(ymod(dy) * nc + ct, h)], cr.at[it, dy, dc - 1, halves[h]],
                        vrc_s.at[dy, dc - 1, h], vrc_r.at[dy, dc - 1, h], at_view(yy, ct),
                    )

    def view_mid(it):
        for dy in list(range(1, ny)) + [0]:
            for h in range(HALVES):
                acc = y[yblock(ymod(dy) * nc + core, h)]
                for dc in range(1, nc):
                    recv(
                        cr.at[it, dy, dc - 1, halves[h]],
                        vrc_s.at[dy, dc - 1, h], vrc_r.at[dy, dc - 1, h],
                        at_view(yy, cmod(-dc)),
                    )
                    acc = acc + cr[it, dy, dc - 1, halves[h]]
                vs[it, dy, halves[h]] = acc
                if dy:
                    send(
                        vs.at[it, dy, halves[h]], yr.at[it, dy, halves[h]],
                        vry_s.at[dy - 1, h], vry_r.at[dy - 1, h], at_view(ymod(dy), core),
                    )

    def view_end(it, h):
        acc = vs[it, 0, halves[h]]
        for dy in range(1, ny):
            recv(
                yr.at[it, dy, halves[h]], vry_s.at[dy - 1, h], vry_r.at[dy - 1, h],
                at_view(ymod(-dy), core),
            )
            acc = acc + yr[it, dy, halves[h]]
        av[it, view, halves[h]] = acc / nview
        own = av.at[it, view, halves[h]]
        for dy in range(1, ny):
            send(
                own, own, vgy_s.at[dy - 1, h], vgy_r.at[dy - 1, h], at_view(ymod(dy), core)
            )
        for dc in range(1, nc):
            send(
                own, own, vgc_s.at[0, dc - 1, h], vgc_r.at[0, dc - 1, h],
                at_view(yy, cmod(dc)),
            )

    def gram_start(it):
        own = av[it, view]
        hi, lo = split(own)
        thi, tlo = split(own.T)
        full = dot3s((thi, tlo), (hi, lo))
        upper = jnp.concatenate([full[:side], full[side:, side:]], axis=1)
        gram[it] = upper.reshape(nrow, gpart, keys + side)
        for d in range(1, nrow):
            to = lax.rem(row + d, nrow)
            send(
                gram.at[it, to], gr.at[it, d], g1_s.at[d - 1], g1_r.at[d - 1], {"row": to}
            )

    def gram_views(it):
        acc = gram[it, row]
        for d in range(1, nrow):
            recv(
                gr.at[it, d], g1_s.at[d - 1], g1_r.at[d - 1],
                {"row": lax.rem(row - d + nrow, nrow)},
            )
            acc = acc + gr[it, d]
        gv[it, 0] = acc
        for d in range(1, nview):
            send(
                gv.at[it, 0], gv.at[it, d], g2_s.at[d - 1], g2_r.at[d - 1],
                {"view": lax.rem(view + d, nview)},
            )

    def gram_rows(it):
        acc = gv[it, 0]
        for d in range(1, nview):
            recv(
                gv.at[it, d], g2_s.at[d - 1], g2_r.at[d - 1],
                {"view": lax.rem(view - d + nview, nview)},
            )
            acc = acc + gv[it, d]
        gfull[it, row] = acc
        mine = gfull.at[it, row]
        for d in range(1, nrow):
            send(
                mine, mine, g3_s.at[d - 1], g3_r.at[d - 1],
                {"row": lax.rem(row + d, nrow)},
            )

    def gram_end(it):
        for d in range(1, nrow):
            src = lax.rem(row - d + nrow, nrow)
            recv(gfull.at[it, src], g3_s.at[d - 1], g3_r.at[d - 1], {"row": src})
        upper = gfull[it].reshape(side, keys + side)
        lower = jnp.concatenate([upper[:, side:keys].T, upper[:, keys:]], axis=1)
        return newton_steps(jnp.concatenate([upper[:, :keys], lower], axis=0))

    def forward_average(it, h):
        for dy in range(1, ny):
            ysrc = ymod(-dy)
            got = av.at[it, ysrc * nc + core, halves[h]]
            recv(got, vgy_s.at[dy - 1, h], vgy_r.at[dy - 1, h], at_view(ysrc, core))
            for dc in range(1, nc):
                send(
                    got, got, vgc_s.at[dy, dc - 1, h], vgc_r.at[dy, dc - 1, h],
                    at_view(yy, cmod(dc)),
                )

    def finish_average(it):
        for dy in range(ny):
            for h in range(HALVES):
                for dc in range(1, nc):
                    csrc = cmod(-dc)
                    recv(
                        av.at[it, ymod(-dy) * nc + csrc, halves[h]],
                        vgc_s.at[dy, dc - 1, h], vgc_r.at[dy, dc - 1, h], at_view(yy, csrc),
                    )

    far = nz - 2
    ns = jax.named_scope
    with ns("q_load"):
        for p in range(cut):
            ag_own(0, p)
        for c in range(nchunk):
            if c + 1 < nchunk:
                load(c + 1).start()
            else:
                shared_load.start()
            load(c).wait()
            for b in range(nrow):
                hi, lo = split(fbuf[c % 2, :, b * shard:(b + 1) * shard])
                fhi[b, c * chunk:(c + 1) * chunk] = hi
                flo[b, c * chunk:(c + 1) * chunk] = lo
            if nchunk - c <= cut:
                ag_event(0, 0, cut - nchunk + c)
    with ns("q_ag0"):
        ag_run(0, True)
    with ns("q_res"):
        shared_load.wait()
        for c in range(local // sub):
            rows = slice(c * sub, (c + 1) * sub)
            put_rt(rows, y[rows] - s_ref[rows])
    with ns("q_rs0c"):
        rs_compute(0)
    with ns("q_rs0e"):
        @pl.loop(0, nz - 1)
        def _(i):
            rs_event(0, far - i)
        ag_flush(0)
        for p in range(cut):
            rows = rows_of[p]
            wf[1, row, rows] = wf[0, row, rows] - step_size * rs_own(0, p)
            ag_own(1, p)
    with ns("q_fl"):
        rs_flush(0)
    with ns("q_ag1"):
        ag_run(1, False)
    with ns("q_vsend"):
        view_send(0)
        for c in range(local // sub):
            rows = slice(c * sub, (c + 1) * sub)
            put_rt(rows, y[rows])
        rs_first(1, 0)
    with ns("q_vmid"):
        view_mid(0)
    with ns("q_rs1c"):
        rs_compute(1, 1)
    with ns("q_rs1e"):
        rs_event(1, far)
    with ns("q_vend"):
        for h in range(HALVES):
            view_end(0, h)
    with ns("q_g1"):
        gram_start(0)
    with ns("q_rs1e"):
        @pl.loop(1, nz - 1)
        def _(i):
            rs_event(1, far - i)
    with ns("q_fa"):
        for h in range(HALVES - 1):
            forward_average(0, h)
    with ns("q_fa"):
        forward_average(0, HALVES - 1)
    with ns("q_fin"):
        finish_average(0)
        ag_flush(1)
        for v in range(nview):
            put_rt(slice(v * part, (v + 1) * part), av[0, v])
    with ns("q_g2"):
        gram_views(0)
    with ns("q_rs2c"):
        rs_first(2, 0)
    with ns("q_g3"):
        gram_rows(0)
    with ns("q_rs2c"):
        rs_compute(2, 1)
    with ns("q_rs1o"):
        for p in range(cut):
            rs_own(1, p)
    with ns("q_rs2e"):
        steps = None
        for i in range(nz - 1):
            rs_event(2, far - i)
            if steps is None and i >= min(1, far):
                with ns("q_nw"):
                    steps = gram_end(0)
                    root, frob = next(steps)
            if steps is not None:
                root, frob = next(steps, (root, frob))
        for root, frob in steps:
            pass
        rootc = split(root.T)
        scale = jnp.sqrt(total / frob)
        for p in range(cut):
            rs_own(2, p)
    with ns("q_w2"):
        moved = dot3s(rootc, split(zs[0, z])) * scale
        wf[0, row] = wf[1, row] - step_size * (zs[1, z] - moved)
        for p in range(cut):
            ag_own(2, p)
        flush()
        rs_flush(1)
        rs_flush(2)
    with ns("q_ag2"):
        ag_run(2, False)
    with ns("q_vmid"):
        view_send(1)
        view_mid(1)
        wo_ref[0] = wf[0, row].T
    with ns("q_vend"):
        for h in range(HALVES):
            view_end(1, h)
    with ns("q_g1"):
        gram_start(1)
        gram_views(1)
    with ns("q_g3"):
        gram_rows(1)
        ag_flush(2)
        for h in range(HALVES):
            forward_average(1, h)
        finish_average(1)
        out = pltpu.make_async_copy(av.at[1], ao_hbm, o_sem)
        out.start()
    with ns("q_g4"):
        steps = gram_end(1)
    with ns("q_nw"):
        for root, frob in steps:
            pass
        root_ref[...] = root * jnp.sqrt(total / frob)
    with ns("q_out"):
        out.wait()
        flush()


def last_product(w_ref, a_ref, root_ref, wo_ref, so_ref):
    @pl.when(pl.program_id(0) == 0)
    def _():
        wo_ref[...] = w_ref[...]

    so_ref[...] = dot3(a_ref[...], root_ref[...])


def solution(mesh):
    nrow, nview = mesh.shape["row"], mesh.shape["view"]
    nx = max(d for d in range(1, math.isqrt(nrow) + 1) if nrow % d == 0)
    nz = nrow // nx
    nc = CORES if nview % CORES == 0 else 1
    ny = nview // nc

    def local(features, view_maps, shared):
        rows, width = features.shape[1], features.shape[2]
        shard, keys = view_maps.shape[1], view_maps.shape[2]
        part, side = rows // nview, keys // 2
        gpart = side // nrow
        cut = CUT
        pieces = [(p * keys // cut, keys // cut) for p in range(cut)]
        chunk = 256
        dma = pltpu.SemaphoreType.DMA
        sems = []
        for shape in [
            (nz + 1, cut), (nz, nx - 1, cut), (2, nz, nx - 1, cut), (2, nz + 1, cut),
            (ny, nc - 1, HALVES), (ny - 1, HALVES), (ny - 1, HALVES), (ny, nc - 1, HALVES),
            (nrow - 1,), (nview - 1,), (nrow - 1,),
        ]:
            sems += [dma(shape), dma(shape)]
        vmem = pl.BlockSpec(memory_space=pltpu.VMEM)
        hbm = pl.BlockSpec(memory_space=pl.ANY)
        maps, average, root = pl.pallas_call(
            functools.partial(kernel, (nz, nx, ny, nc), pieces),
            out_shape=(
                jax.ShapeDtypeStruct(view_maps.shape, F32),
                jax.ShapeDtypeStruct((nview, part, keys), F32),
                jax.ShapeDtypeStruct((keys, keys), F32),
            ),
            in_specs=[hbm, vmem, hbm],
            out_specs=(vmem, hbm, vmem),
            scratch_shapes=[
                pltpu.VMEM((rows, keys), F32),
                pltpu.VMEM((nrow, rows, shard), BF16),
                pltpu.VMEM((nrow, rows, shard), BF16),
                pltpu.VMEM((2, chunk, width), F32),
                pltpu.VMEM((keys, rows), BF16),
                pltpu.VMEM((keys, rows), BF16),
                pltpu.VMEM((rows, keys), F32),
                pltpu.VMEM((2, nrow, keys, shard), F32),
                pltpu.VMEM((2, nz, nx - 1, keys, shard), F32),
                pltpu.VMEM((2, nz, nx - 1, keys, shard), F32),
                pltpu.VMEM((2, nz, keys, shard), F32),
                pltpu.VMEM((2, nz + 1, keys, shard), F32),
                pltpu.VMEM((ITERS, ny, part, keys), F32),
                pltpu.VMEM((ITERS, ny, nc - 1, part, keys), F32),
                pltpu.VMEM((ITERS, ny, part, keys), F32),
                pltpu.VMEM((ITERS, nview, part, keys), F32),
                pltpu.VMEM((ITERS, nrow, gpart, keys + side), F32),
                pltpu.VMEM((ITERS, nrow, gpart, keys + side), F32),
                pltpu.VMEM((ITERS, nview, gpart, keys + side), F32),
                pltpu.VMEM((ITERS, nrow, gpart, keys + side), F32),
                dma((2,)), dma, dma,
            ] + sems,
            compiler_params=pltpu.CompilerParams(
                collective_id=0, has_side_effects=True, vmem_limit_bytes=67043328
            ),
        )(features, view_maps, shared)
        whole = pl.BlockSpec((1, shard, keys), lambda c: (0, 0, 0))
        span = rows // LAST
        tile = pl.BlockSpec((span, keys), lambda c: (c, 0))
        return pl.pallas_call(
            last_product,
            grid=(LAST,),
            out_shape=(
                jax.ShapeDtypeStruct(view_maps.shape, F32),
                jax.ShapeDtypeStruct(shared.shape, F32),
            ),
            in_specs=[whole, tile, pl.BlockSpec((keys, keys), lambda c: (0, 0))],
            out_specs=(whole, tile),
        )(maps, average.reshape(rows, keys), root)

    in_specs = (P("view", "row", None), P("view", "row", None), P("row", None))
    out_specs = (P("view", "row", None), P("row", None))
    return jax.shard_map(local, mesh=mesh, in_specs=in_specs, out_specs=out_specs, check_vma=False)
```
